256 devices in a mesh: width: 8 (over y, core), hidden: 32 (over z, x).
Axes of the slice: x: 4, y: 4, z: 8, core: 2. Of those that a mesh axis runs over, the one named last changes fastest.
Arguments:
- tokens: bfloat16 [1152, 5120], P(None, 'width'), may hold values from -6 to 6
- cotangent: bfloat16 [1152, 5120], P(None, 'width'), may hold values from -6 to 6
- w_up: bfloat16 [5120, 13824], P('width', 'hidden'), may hold values from -0.078125 to 0.078125
- bias_up: float32 [13824], P('hidden'), may hold values from -3 to 3
- w_down: bfloat16 [13824, 5120], P('hidden', 'width'), may hold values from -0.0546875 to 0.0546875
- mod_table: float32 [32, 3, 5120], P(None, None, 'width'), may hold values from -3 to 3
- seg_ids: int32 [1152], replicated, may hold values from 0 to 15, never falling along the last dimension, each value on 1 to 144 neighbouring positions
- step_ids: int32 [16], replicated, may hold values from 0 to 31
Outputs:
- grad_x: bfloat16 [1152, 5120], P(None, 'width')
- grad_up: float32 [5120, 13824], P('width', 'hidden')
- grad_down: float32 [13824, 5120], P('hidden', 'width')
- grad_bias: float32 [13824], P('hidden')
- grad_table: float32 [32, 3, 5120], P(None, None, 'width')
The draws below stay inside these ranges and needn't reach their ends.
Inputs may be any that keep to these rules, and one draw needn't show every extreme that they name: `seg_ids`: request numbers never fall along the tokens and every request holds at least one token.
All inputs are finite; a program needn't handle non-finite values.
Results may differ from the reference program's by a relative error of at most 0.0063.
Values may be sent and summed in bfloat16 or wider, within the bound.
A program may use at most 64 MiB of HBM per device.

```python
import math
import jax
import jax.numpy as jnp
import numpy as np
from jax import lax

D = 5120
FF = 13824
TOKENS = 1152
REQUESTS = 16
NSTEPS = 32


def plant(array, rng, smallest, high):
    spot = [jax.random.randint(jax.random.fold_in(rng, axis), (), 0, length) for axis, length in enumerate(array.shape)]
    widest = array.shape.index(max(array.shape))
    next_to = spot[:widest] + [(spot[widest] + 1) % array.shape[widest]] + spot[widest + 1:]
    return array.at[tuple(spot)].set(smallest).at[tuple(next_to)].set(high)


def block_scale(rng, shape, split, smallest, top_value):
    def one(position, parts):
        heights = jax.random.uniform(jax.random.fold_in(jax.random.fold_in(rng, 6), position), (parts,), jnp.float32, smallest / len(split), top_value / len(split))
        return jnp.repeat(jnp.exp(heights), shape[position] // parts).reshape((-1,) + (1,) * (len(shape) - position - 1))

    factor_of = one(*split[0])
    for cut in split[1:]:
        factor_of = factor_of * one(*cut)
    return factor_of


def length_profile(amount, total, limit, lean):
    loads = [(1 << 20) // math.isqrt(grade ** lean) + 1 for grade in range(2, amount + 1)]
    rest, counts = total - limit - (amount - 1), [1] * (amount - 1)
    while rest > 0:
        movable = [i for i in range(amount - 1) if counts[i] < limit]
        whole, left = sum([loads[i] for i in movable]), rest
        for i in movable:
            addition = min(limit - counts[i], max(1, left * loads[i] // whole), rest)
            counts[i] = counts[i] + addition
            rest = rest - addition
    return np.array([limit] + counts)


def ragged_sizes(stream_key, count, total, limit, skew):
    if count == 2:
        one = jax.random.randint(stream_key, (), max(1, total - limit), min(limit, total - 1) + 1)
        return jnp.stack([one, total - one])
    lengths = jnp.asarray(length_profile(count, total, limit, skew), jnp.int32)
    pairs = (count - 1) // 2
    giver, taker = lengths[1:1 + 2 * pairs:2], lengths[2:2 + 2 * pairs:2]
    slack = jnp.minimum(giver - 1, limit - taker)
    shifted = jax.random.randint(jax.random.fold_in(stream_key, 1), (pairs,), 0, 1 << 20) % (slack + 1)
    lengths = lengths.at[1:1 + 2 * pairs:2].set(giver - shifted).at[2:2 + 2 * pairs:2].set(taker + shifted)
    return lengths[jax.random.permutation(jax.random.fold_in(stream_key, 2), count)]


def bell_draw(rng, extent, width, limit, cuts=(), dtype=jnp.bfloat16):
    entries = width * jax.random.normal(rng, extent, jnp.float32)
    if cuts:
        entries = entries * block_scale(rng, extent, cuts, -0.22, 0.18)
    return jnp.clip(entries, -limit, limit).astype(dtype)


def setup_inputs(seed: int = 0) -> dict:
    key_list = jax.random.split(jax.random.key(seed), 9)
    tokens = bell_draw(key_list[0], (TOKENS, D), 1.0, 6.0, ((1, 8),))
    cotangent = bell_draw(key_list[1], (TOKENS, D), 1.0, 6.0, ((1, 8),))
    w_up = bell_draw(key_list[2], (D, FF), D ** -0.5, 0.078125, ((0, 8), (1, 32)))
    bias_up = bell_draw(key_list[3], (FF,), 0.5, 3.0, ((0, 32),), jnp.float32)
    w_down = bell_draw(key_list[4], (FF, D), FF ** -0.5, 0.0546875, ((0, 32), (1, 8)))
    mod_table = bell_draw(key_list[5], (NSTEPS, 3, D), 0.5, 3.0, ((2, 8),), jnp.float32)
    seg_ids = jnp.searchsorted(jnp.cumsum(ragged_sizes(key_list[6], REQUESTS, TOKENS, TOKENS // 8, 1)), jnp.arange(TOKENS), side="right").astype(jnp.int32)
    step_ids = plant(jax.random.randint(key_list[7], (REQUESTS,), 0, NSTEPS), jax.random.fold_in(key_list[7], 1), 0, NSTEPS - 1).astype(jnp.int32)
    return {"tokens": tokens, "cotangent": cotangent, "w_up": w_up, "bias_up": bias_up, "w_down": w_down, "mod_table": mod_table, "seg_ids": seg_ids, "step_ids": step_ids}


def gelu_tanh(value):
    return jax.nn.gelu(value, approximate=True)

def reference(tokens, cotangent, w_up, bias_up, w_down, mod_table, seg_ids, step_ids):
    highest = lax.Precision.HIGHEST
    req_of = (seg_ids[:, None] == jnp.arange(REQUESTS)[None, :]).astype(jnp.float32)
    step_of = (step_ids[:, None] == jnp.arange(NSTEPS)[None, :]).astype(jnp.float32)
    req_mod = jnp.einsum('rk,kcd->rcd', step_of, mod_table, precision=highest)
    shift_tok = jnp.dot(req_of, req_mod[:, 0], precision=highest)
    scale_tok = jnp.dot(req_of, req_mod[:, 1], precision=highest)
    gate_tok = jnp.dot(req_of, req_mod[:, 2], precision=highest)
    x_full = tokens.astype(jnp.float32)
    tok_mean = lax.optimization_barrier(jnp.sum(x_full, 1)) / D
    tok_var = lax.optimization_barrier(jnp.sum(x_full * x_full, 1)) / D - tok_mean * tok_mean
    inv_std = lax.rsqrt(tok_var + 1e-06)
    x_hat = (x_full - tok_mean[:, None]) * inv_std[:, None]
    mod_gain = 1.0 + scale_tok
    normed = (x_hat * mod_gain + shift_tok).astype(jnp.bfloat16)
    pre_act = jnp.dot(normed, w_up, preferred_element_type=jnp.float32) + bias_up
    hidden_act = gelu_tanh(pre_act).astype(jnp.bfloat16)
    y_out = jnp.dot(hidden_act, w_down, preferred_element_type=jnp.float32)
    grad_gate_req = jnp.dot(req_of.T, cotangent.astype(jnp.float32) * y_out, precision=highest)
    d_out = (cotangent.astype(jnp.float32) * gate_tok).astype(jnp.bfloat16)
    d_act = jnp.dot(d_out, w_down.T, preferred_element_type=jnp.float32)
    _, pull = jax.vjp(gelu_tanh, pre_act)
    d_pre = pull(d_act)[0]
    d_pre_b = d_pre.astype(jnp.bfloat16)
    grad_bias = lax.optimization_barrier(jnp.sum(d_pre, 0))
    grad_down = jnp.dot(hidden_act.T, d_out, preferred_element_type=jnp.float32)
    grad_up = jnp.dot(normed.T, d_pre_b, preferred_element_type=jnp.float32)
    d_norm = jnp.dot(d_pre_b, w_up.T, preferred_element_type=jnp.float32)
    grad_shift_req = jnp.dot(req_of.T, d_norm, precision=highest)
    grad_scale_req = jnp.dot(req_of.T, d_norm * x_hat, precision=highest)
    req_grads = jnp.stack([grad_shift_req, grad_scale_req, grad_gate_req], 1)
    grad_table = jnp.einsum('rk,rcd->kcd', step_of, req_grads, precision=highest)
    d_hat = d_norm * mod_gain
    mean_one = lax.optimization_barrier(jnp.sum(d_hat, 1)) / D
    mean_two = lax.optimization_barrier(jnp.sum(d_hat * x_hat, 1)) / D
    grad_x = cotangent.astype(jnp.float32) + inv_std[:, None] * (d_hat - mean_one[:, None] - x_hat * mean_two[:, None])
    return (grad_x.astype(jnp.bfloat16), grad_up, grad_down, grad_bias, grad_table)
```

```python
import functools

import jax
import jax.numpy as jnp
from jax import lax
from jax.experimental import pallas as pl
from jax.experimental.pallas import tpu as pltpu
from jax.sharding import PartitionSpec as P

MESH = pl.DeviceIdType.MESH
F32, BF16 = jnp.float32, jnp.bfloat16

T, DW, FW, R, NS = 1152, 640, 432, 16, 32
D = 5120
CH = 144
HALF = 576
OWN = 48
CUT = 384
ROOT = 0.7978845608028654
CUBE = 0.044715


def split3(v):
    hi = v.astype(BF16)
    rest = v - hi.astype(F32)
    mid = rest.astype(BF16)
    return hi, mid, (rest - mid.astype(F32)).astype(BF16)


def dot(a, b, dims=((1,), (0,))):
    return lax.dot_general(a, b, (dims, ((), ())), preferred_element_type=F32)


def rows_at(start, size, step=16):
    return pl.ds(pl.multiple_of(start, step), size)


def kernel(
    tok, cot, wup, bias, wdn, tab, seg, stp,
    gx, gup, gdn, gb, gtab,
    stat, rmod, oh, oht, col, dout, nrm,
    psib, rsib, pown, ysum, yrec, had,
    dn, sb, rb, zsum, xs, xr, mst,
    tl, tx, ts, tz, tf,
    st_s, st_r, cx_s, cx_r, yr_s, yr_r, ya_s, ya_r, fw_s, fw_r,
    zr_s, zr_r, xe_s, xe_r, ms_s, ms_r, xg_s, xg_r, zg_s, zg_r,
    tx_s, tx_r, tz_s, tz_r, tg_s, tg_r,
):
    w = lax.axis_index("width")
    h = lax.axis_index("hidden")
    y, c = w // 2, w % 2
    z, x = h // 4, h % 4

    def at_w(d):
        return ((w + d) % 8, h)

    def at_y(d):
        return (((y + d) % 4) * 2 + c, h)

    sib = (y * 2 + 1 - c, h)

    def at_z(d):
        return (w, ((z + d) % 8) * 4 + x)

    def at_x(d):
        return (w, z * 4 + (x + d) % 4)

    def send(src, dst, s_sem, r_sem, dev):
        return pltpu.make_async_remote_copy(
            src_ref=src, dst_ref=dst, send_sem=s_sem, recv_sem=r_sem, device_id=dev, device_id_type=MESH
        )

    bar = pltpu.get_barrier_semaphore()
    for d in range(1, 8):
        pl.semaphore_signal(bar, inc=1, device_id=at_w(d), device_id_type=MESH)
        pl.semaphore_signal(bar, inc=1, device_id=at_z(d), device_id_type=MESH)
    for d in range(1, 4):
        pl.semaphore_signal(bar, inc=1, device_id=at_x(d), device_id_type=MESH)

    @pl.loop(0, 9)
    def _(b):
        v = tok[rows_at(b * 128, 128, 128), :].astype(F32)
        s1 = v[:, 0:128]
        s2 = v[:, 0:128] * v[:, 0:128]
        for k in range(1, 5):
            p = v[:, k * 128 : (k + 1) * 128]
            s1 = s1 + p
            s2 = s2 + p * p
        lanes = rows_at(b * 128, 128, 128)
        stat[w, 0:1, lanes] = jnp.sum(s1.T, 0, keepdims=True)
        stat[w, 1:2, lanes] = jnp.sum(s2.T, 0, keepdims=True)

    pl.semaphore_wait(bar, 17)

    st_cp = [send(stat.at[w], stat.at[w], st_s.at[d - 1], st_r.at[d - 1], at_w(d)) for d in range(1, 8)]
    for cp in st_cp:
        cp.start()

    step_of = (stp[...] == lax.broadcasted_iota(jnp.int32, (R, NS), 1)).astype(F32).astype(BF16)
    for k in range(3):
        parts = split3(tab[:, k, :])
        rm = dot(step_of, parts[0]) + dot(step_of, parts[1]) + dot(step_of, parts[2])
        for i, part in enumerate(split3(rm)):
            rmod[k, i * R : (i + 1) * R, :] = part
    oht[...] = (seg[...] == lax.broadcasted_iota(jnp.int32, (R, T), 0)).astype(F32).astype(BF16)

    @pl.loop(0, 9)
    def _(b):
        lanes = rows_at(b * 128, 128, 128)
        one = (seg[:, lanes] == lax.broadcasted_iota(jnp.int32, (R, 128), 0)).astype(F32)
        three = jnp.concatenate([one, one, one], 0)
        oh[lanes, :] = three.T.astype(BF16)
        gate = dot(oh[lanes, :], rmod[2])
        dout[lanes, :] = (cot[lanes, :].astype(F32) * gate).astype(BF16)

    def width_reduce(a, left, right, dims):
        @pl.loop(0, 2)
        def _(k):
            p = dot(left[rows_at((1 - c) * HALF + k * 288, 288), :], right[...], dims).astype(BF16)
            psib[a, 2 * k] = p[0:CH]
            psib[a, 2 * k + 1] = p[CH:288]

        cx = send(psib.at[a], rsib.at[a], cx_s.at[a], cx_r.at[a], sib)
        cx.start()

        @pl.loop(0, 2)
        def _(k):
            p = dot(left[rows_at(c * HALF + k * 288, 288), :], right[...], dims)
            pown[2 * k] = p[0:CH]
            pown[2 * k + 1] = p[CH:288]

        cx.wait()

        @pl.loop(0, 4)
        def _(k):
            ysum[a, k] = (pown[k] + rsib[a, k].astype(F32)).astype(BF16)

        cps = []
        for d in (2, 1, 3):
            cp = send(ysum.at[a, (y + d) % 4], yrec.at[a, d - 1], yr_s.at[a, d - 1], yr_r.at[a, d - 1], at_y(d))
            cp.start()
            cps.append(cp)
        return cps

    y_cps = width_reduce(0, dout, wdn, ((1,), (1,)))

    for cp in st_cp:
        cp.wait()
    tot = stat[0]
    for k in range(1, 8):
        tot = tot + stat[k]
    mu = tot[0:1] / D
    inv = lax.rsqrt(tot[1:2] / D - mu * mu + 1e-06)
    mu8 = jnp.broadcast_to(mu, (8, T))
    inv8 = jnp.broadcast_to(inv, (8, T))
    for b in range(9):
        lanes = slice(b * 128, (b + 1) * 128)
        col[0, lanes, :] = mu8[:, lanes].T
        col[1, lanes, :] = inv8[:, lanes].T

    @pl.loop(0, 9)
    def _(b):
        rows = rows_at(b * 128, 128, 128)
        shift = dot(oh[rows, :], rmod[0])
        gain = 1.0 + dot(oh[rows, :], rmod[1])
        xh = (tok[rows, :].astype(F32) - col[0, rows, 0:1]) * col[1, rows, 0:1]
        nrm[rows, :] = (xh * gain + shift).astype(BF16)

    y_cps = y_cps + width_reduce(1, nrm, wup, ((1,), (0,)))
    for cp in y_cps:
        cp.wait()

    def width_total(a):
        v = ysum[a, y].astype(F32)
        for d in range(3):
            v = v + yrec[a, d].astype(F32)
        return v

    pre = width_total(1) + bias[...]
    sq = pre * pre
    th = jnp.tanh(ROOT * (pre + CUBE * (sq * pre)))
    mine = rows_at(c * HALF + y * CH, CH)
    had[0, mine, :] = (0.5 * pre * (1.0 + th)).astype(BF16)
    slope = 0.5 * (1.0 + th) + (0.5 * ROOT) * pre * (1.0 - th * th) * (1.0 + (3.0 * CUBE) * sq)
    had[1, mine, :] = (width_total(0) * slope).astype(BF16)

    def chunk(k, q):
        return had.at[:, rows_at(k * HALF + q * CH, CH), :]

    ya = {}
    for d in (2, 1, 3):
        ya[d] = send(chunk(c, y), chunk(c, y), ya_s.at[d - 1], ya_r.at[d - 1], at_y(d))
        ya[d].start()
    fw = [send(chunk(c, y), chunk(c, y), fw_s.at[0], fw_r.at[0], sib)]
    fw[0].start()
    for d in (1, 3, 2):
        ya[d].wait()
        src = chunk(c, (y + 4 - d) % 4)
        cp = send(src, src, fw_s.at[d], fw_r.at[d], sib)
        cp.start()
        fw.append(cp)
    for cp in fw:
        cp.wait()

    def zrows(d):
        return rows_at(((z + d) % 8) * CH, CH)

    def part(d):
        dn[zrows(d), :] = dot(had[1, zrows(d), :], wup[...], ((1,), (1,)))

    def hop(step, lanes_p, lanes_m):
        cps = []
        for k, (lanes, to) in enumerate(((lanes_p, 1), (lanes_m, 7))):
            cp = send(sb.at[k, step, :, lanes], rb.at[k, step, :, lanes], zr_s.at[k, step], zr_r.at[k, step], at_z(to))
            cp.start()
            cps.append(cp)
        return cps

    full = pl.ds(0, DW)
    part(4)
    far = dn[zrows(4), :].astype(BF16)
    sb[0, 0, :, 0:CUT] = far[:, 0:CUT]
    sb[1, 0, :, CUT:DW] = far[:, CUT:DW]
    zr = hop(0, pl.ds(0, CUT), pl.ds(CUT, DW - CUT))
    part(3)
    part(5)
    for cp in zr:
        cp.wait()
    sb[0, 1, :, 0:CUT] = (dn[zrows(3), 0:CUT] + rb[0, 0, :, 0:CUT].astype(F32)).astype(BF16)
    sb[0, 1, :, CUT:DW] = dn[zrows(3), CUT:DW].astype(BF16)
    sb[1, 1, :, 0:CUT] = dn[zrows(5), 0:CUT].astype(BF16)
    sb[1, 1, :, CUT:DW] = (dn[zrows(5), CUT:DW] + rb[1, 0, :, CUT:DW].astype(F32)).astype(BF16)
    zr = hop(1, full, full)
    part(2)
    part(6)
    part(1)
    part(7)
    part(0)
    for cp in zr:
        cp.wait()
    sb[0, 2] = (dn[zrows(2), :] + rb[0, 1].astype(F32)).astype(BF16)
    sb[1, 2] = (dn[zrows(6), :] + rb[1, 1].astype(F32)).astype(BF16)
    zr = hop(2, full, full)

    def table_block(b, carry):
        rows = rows_at(b * 128, 128, 128)
        dv = dn[rows, :]
        xh = (tok[rows, :].astype(F32) - col[0, rows, 0:1]) * col[1, rows, 0:1]
        yv = dot(had[0, rows, :], wdn[...]) * cot[rows, :].astype(F32)
        hot = oht[:, rows]
        out = []
        for acc, v in zip(carry, (dv, dv * xh, yv)):
            hi = v.astype(BF16)
            lo = (v - hi.astype(F32)).astype(BF16)
            out.append(acc + dot(hot, hi) + dot(hot, lo))
        return tuple(out)

    zero = jnp.zeros((R, DW), F32)
    sums = lax.fori_loop(0, 9, table_block, (zero, zero, zero))
    for k in range(3):
        tx[x, 2 * k] = sums[k][0:8]
        tx[x, 2 * k + 1] = sums[k][8:16]
    tcp = [send(tx.at[x], tx.at[x], tx_s.at[d - 1], tx_r.at[d - 1], at_x(d)) for d in range(1, 4)]
    for cp in tcp:
        cp.start()

    for cp in zr:
        cp.wait()
    sb[0, 3] = (dn[zrows(1), :] + rb[0, 2].astype(F32)).astype(BF16)
    sb[1, 3] = (dn[zrows(7), :] + rb[1, 2].astype(F32)).astype(BF16)
    zr = hop(3, full, full)

    for cp in tcp:
        cp.wait()
    ts[...] = (tx[0] + tx[1]) + (tx[2] + tx[3])
    for d in range(1, 8):
        @pl.when((z + d) % 8 < 6)
        def _():
            send(ts.at[(z + d) % 8], tz.at[z], tz_s.at[d - 1], tz_r.at[d - 1], at_z(d)).start()

    for m in range(4):
        n = min(128, FW - m * 128)
        gdn[m * 128 : m * 128 + n, :] = dot(had[0, :, m * 128 : m * 128 + n], dout[...], ((0,), (0,)))

    for cp in zr:
        cp.wait()
    zsum[...] = dn[zrows(0), :] + rb[0, 3].astype(F32) + rb[1, 3].astype(F32)
    for k in range(3):
        xs[k] = zsum[k * OWN : (k + 1) * OWN, :].astype(BF16)
    for d in range(1, 4):
        @pl.when((x + d) % 4 < 3)
        def _():
            send(xs.at[(x + d) % 4], xr.at[d - 1], xe_s.at[d - 1], xe_r.at[d - 1], at_x(d)).start()

    for d in range(1, 8):
        @pl.when((z + d) % 8 < 6)
        def _():
            send(ts.at[(z + d) % 8], tz.at[z], tz_s.at[d - 1], tz_r.at[d - 1], at_z(d)).wait_send()

    @pl.when(z < 6)
    def _():
        for d in range(1, 8):
            send(ts.at[0], tz.at[(z + 8 - d) % 8], tz_s.at[d - 1], tz_r.at[d - 1], at_z(d)).wait_recv()
        tz[z] = ts[z]
        v = tz[0]
        for k in range(1, 8):
            v = v + tz[k]
        tf[z] = v
        for d in range(1, 8):
            send(tf.at[z], tf.at[z], tg_s.at[d - 1], tg_r.at[d - 1], at_z(d)).start()

    for d in range(1, 4):
        @pl.when((x + d) % 4 < 3)
        def _():
            send(xs.at[(x + d) % 4], xr.at[d - 1], xe_s.at[d - 1], xe_r.at[d - 1], at_x(d)).wait_send()

    @pl.when(x < 3)
    def _():
        for d in range(1, 4):
            send(xs.at[0], xr.at[d - 1], xe_s.at[d - 1], xe_r.at[d - 1], at_x(d)).wait_recv()
        v = zsum[rows_at(x * OWN, OWN), :]
        for d in range(3):
            v = v + xr[d].astype(F32)
        rows = rows_at(z * CH + x * OWN, OWN)
        gain = 1.0 + dot(oh[rows, :], rmod[1])
        rstd = col[1, rows, 0:1]
        xh = (tok[rows, :].astype(F32) - col[0, rows, 0:1]) * rstd
        dh = v * gain
        dhx = dh * xh
        s1 = dh[:, 0:128]
        s2 = dhx[:, 0:128]
        for k in range(1, 5):
            s1 = s1 + dh[:, k * 128 : (k + 1) * 128]
            s2 = s2 + dhx[:, k * 128 : (k + 1) * 128]
        s1 = jnp.sum(s1, 1, keepdims=True)
        s2 = jnp.sum(s2, 1, keepdims=True)
        lane = lax.broadcasted_iota(jnp.int32, (OWN, 128), 1)
        mst[w] = jnp.where(lane < 64, s1, s2)
        cps = [send(mst.at[w], mst.at[w], ms_s.at[d - 1], ms_r.at[d - 1], at_w(d)) for d in range(1, 8)]
        for cp in cps:
            cp.start()
        for cp in cps:
            cp.wait()
        m = mst[0]
        for k in range(1, 8):
            m = m + mst[k]
        m = m / D
        grad = cot[rows, :].astype(F32) + rstd * (dh - m[:, 0:1] - xh * m[:, 64:65])
        gx[rows, :] = grad.astype(BF16)
        for d in range(1, 4):
            send(gx.at[rows], gx.at[rows], xg_s.at[d - 1], xg_r.at[d - 1], at_x(d)).start()
        for d in range(1, 4):
            send(gx.at[rows], gx.at[rows], xg_s.at[d - 1], xg_r.at[d - 1], at_x(d)).wait_send()

    for d in range(1, 4):
        @pl.when((x + 4 - d) % 4 < 3)
        def _():
            rows = rows_at(z * CH + ((x + 4 - d) % 4) * OWN, OWN)
            send(gx.at[rows], gx.at[rows], xg_s.at[d - 1], xg_r.at[d - 1], at_x(d)).wait_recv()

    def spread(step, lanes_p, lanes_m):
        cps = []
        for k, (lanes, to, src) in enumerate(((lanes_p, 1, 8 - step), (lanes_m, 7, step))):
            ref = gx.at[zrows(src), lanes]
            cp = send(ref, ref, zg_s.at[k, step], zg_r.at[k, step], at_z(to))
            cp.start()
            cps.append(cp)
        return cps

    zg = spread(0, full, full)

    @pl.loop(0, 5)
    def _(m):
        lanes = rows_at(m * 128, 128, 128)
        gup[lanes, :] = dot(nrm[:, lanes], had[1], ((0,), (0,)))

    gb[...] = dot(jnp.ones((8, T), BF16), had[1])[0:1]

    for cp in zg:
        cp.wait()
    zg = spread(1, full, full)

    for d in range(1, 8):
        @pl.when(z < 6)
        def _():
            send(tf.at[z], tf.at[z], tg_s.at[d - 1], tg_r.at[d - 1], at_z(d)).wait_send()

        @pl.when((z + 8 - d) % 8 < 6)
        def _():
            k = (z + 8 - d) % 8
            send(tf.at[k], tf.at[k], tg_s.at[d - 1], tg_r.at[d - 1], at_z(d)).wait_recv()

    for k in range(3):
        v = jnp.concatenate([tf[2 * k], tf[2 * k + 1]], 0)
        out = jnp.zeros((NS, DW), F32)
        for p in split3(v):
            out = out + dot(step_of, p, ((0,), (0,)))
        gtab[:, k, :] = out

    for cp in zg:
        cp.wait()
    zg = spread(2, full, full)
    for cp in zg:
        cp.wait()
    zg = spread(3, pl.ds(0, CUT), pl.ds(CUT, DW - CUT))
    for cp in zg:
        cp.wait()


def per_device(tokens, cotangent, w_up, bias_up, w_down, mod_table, seg_ids, step_ids):
    vm = pl.BlockSpec(memory_space=pltpu.VMEM)
    dma = pltpu.SemaphoreType.DMA
    outs = pl.pallas_call(
        kernel,
        out_shape=(
            jax.ShapeDtypeStruct((T, DW), BF16),
            jax.ShapeDtypeStruct((DW, FW), F32),
            jax.ShapeDtypeStruct((FW, DW), F32),
            jax.ShapeDtypeStruct((1, FW), F32),
            jax.ShapeDtypeStruct((NS, 3, DW), F32),
        ),
        in_specs=[vm] * 8,
        out_specs=(vm,) * 5,
        scratch_shapes=[
            pltpu.VMEM((8, 2, T), F32),
            pltpu.VMEM((3, 3 * R, DW), BF16),
            pltpu.VMEM((T, 3 * R), BF16),
            pltpu.VMEM((R, T), BF16),
            pltpu.VMEM((2, T, 8), F32),
            pltpu.VMEM((T, DW), BF16),
            pltpu.VMEM((T, DW), BF16),
            pltpu.VMEM((2, 4, CH, FW), BF16),
            pltpu.VMEM((2, 4, CH, FW), BF16),
            pltpu.VMEM((4, CH, FW), F32),
            pltpu.VMEM((2, 4, CH, FW), BF16),
            pltpu.VMEM((2, 3, CH, FW), BF16),
            pltpu.VMEM((2, T, FW), BF16),
            pltpu.VMEM((T, DW), F32),
            pltpu.VMEM((2, 4, CH, DW), BF16),
            pltpu.VMEM((2, 4, CH, DW), BF16),
            pltpu.VMEM((CH, DW), F32),
            pltpu.VMEM((3, OWN, DW), BF16),
            pltpu.VMEM((3, OWN, DW), BF16),
            pltpu.VMEM((8, OWN, 128), F32),
            pltpu.VMEM((8, DW), F32),
            pltpu.VMEM((4, 6, 8, DW), F32),
            pltpu.VMEM((6, 8, DW), F32),
            pltpu.VMEM((8, 8, DW), F32),
            pltpu.VMEM((6, 8, DW), F32),
            dma((7,)), dma((7,)),
            dma((2,)), dma((2,)),
            dma((2, 3)), dma((2, 3)),
            dma((3,)), dma((3,)),
            dma((4,)), dma((4,)),
            dma((2, 4)), dma((2, 4)),
            dma((3,)), dma((3,)),
            dma((7,)), dma((7,)),
            dma((3,)), dma((3,)),
            dma((2, 4)), dma((2, 4)),
            dma((3,)), dma((3,)),
            dma((7,)), dma((7,)),
            dma((7,)), dma((7,)),
        ],
        compiler_params=pltpu.CompilerParams(
            collective_id=0, has_side_effects=True, vmem_limit_bytes=56 * 1024 * 1024
        ),
        name="mlp_backward",
    )(
        tokens, cotangent, w_up, bias_up[None, :], w_down, mod_table, seg_ids[None, :], step_ids[:, None]
    )
    return outs[0], outs[1], outs[2], outs[3][0], outs[4]


def solution(mesh):
    placed = (
        P(None, "width"),
        P(None, "width"),
        P("width", "hidden"),
        P("hidden"),
        P("hidden", "width"),
        P(None, None, "width"),
        P(),
        P(),
    )
    return jax.shard_map(
        per_device,
        mesh=mesh,
        in_specs=placed,
        out_specs=(
            P(None, "width"),
            P("width", "hidden"),
            P("hidden", "width"),
            P("hidden"),
            P(None, None, "width"),
        ),
        check_vma=False,
    )
```

```python
import functools

import jax
import jax.numpy as jnp
from jax import lax
from jax.experimental import pallas as pl
from jax.experimental.pallas import tpu as pltpu
from jax.sharding import PartitionSpec as P

MESH = pl.DeviceIdType.MESH
F32, BF16 = jnp.float32, jnp.bfloat16

T, DW, FW, R, NS = 1152, 640, 432, 16, 32
D = 5120
NB = 3
BLK = 384
OWN = 48
HALF = 192
CUT = 384
ROOT = 0.7978845608028654
CUBE = 0.044715


def split3(v):
    hi = v.astype(BF16)
    rest = v - hi.astype(F32)
    mid = rest.astype(BF16)
    return hi, mid, (rest - mid.astype(F32)).astype(BF16)


def dot(a, b, dims=((1,), (0,))):
    return lax.dot_general(a, b, (dims, ((), ())), preferred_element_type=F32)


def rows_at(start, size, step=16):
    return pl.ds(pl.multiple_of(start, step), size)


def kernel(
    tok_h, cot_h, wup_h, bias, wdn_h, tab, seg, stp,
    gx, gup_h, gdn_h, gb, gtab,
    tok, cot, wup, wdn, gup, gdn,
    stat, rmod, oh, oht, col, dout, nrm,
    psib, rsib, pown, ysum, yrec, had,
    dn, sb, rb, zsum, xs, xr, dhv, mst,
    tx, tz, tf, comp,
    in_s, out_s, st_s, st_r, cx_s, cx_r, yd_s, yd_r, yu_s, yu_r, ya_s, ya_r, fw_s, fw_r,
    ha_s, ha_r, hf_s, hf_r, zr_s, zr_r, xe_s, xe_r, ms_s, ms_r, xg_s, xg_r, zg_s, zg_r,
    tx_s, tx_r, tz_s, tz_r, tg_s, tg_r, tb_s, tb_r,
):
    w = lax.axis_index("width")
    h = lax.axis_index("hidden")
    y, c = w // 2, w % 2
    z, x = h // 4, h % 4
    me = c * 4 + y

    def at_w(d):
        return ((w + d) % 8, h)

    def at_y(d):
        return (((y + d) % 4) * 2 + c, h)

    sib = (y * 2 + 1 - c, h)

    def at_z(d):
        return (w, ((z + d) % 8) * 4 + x)

    def at_x(d):
        return (w, z * 4 + (x + d) % 4)

    def send(src, dst, s_sem, r_sem, dev):
        return pltpu.make_async_remote_copy(
            src_ref=src, dst_ref=dst, send_sem=s_sem, recv_sem=r_sem, device_id=dev, device_id_type=MESH
        )

    loads = {}
    for i, (name, src, dst) in enumerate(
        (("tok", tok_h, tok), ("cot", cot_h, cot), ("wdn", wdn_h, wdn), ("wup", wup_h, wup))
    ):
        loads[name] = pltpu.make_async_copy(src, dst, in_s.at[i])
        loads[name].start()

    bar = pltpu.get_barrier_semaphore()
    for d in range(1, 8):
        pl.semaphore_signal(bar, inc=1, device_id=at_w(d), device_id_type=MESH)
        pl.semaphore_signal(bar, inc=1, device_id=at_z(d), device_id_type=MESH)
    for d in range(1, 4):
        pl.semaphore_signal(bar, inc=1, device_id=at_x(d), device_id_type=MESH)

    row = lax.broadcasted_iota(jnp.int32, (R, NS), 0)
    picked = jnp.zeros((R, NS), jnp.int32)
    for r in range(R):
        picked = jnp.where(row == r, stp[r], picked)
    step_of = (picked == lax.broadcasted_iota(jnp.int32, (R, NS), 1)).astype(F32).astype(BF16)
    for k in range(3):
        parts = split3(tab[k])
        rm = dot(step_of, parts[0]) + dot(step_of, parts[1]) + dot(step_of, parts[2])
        for i, part in enumerate(split3(rm)):
            rmod[k, i * R : (i + 1) * R, :] = part

    loads["tok"].wait()

    @pl.loop(0, 9)
    def _(b):
        v = tok[rows_at(b * 128, 128, 128), :].astype(F32)
        s1 = v[:, 0:128]
        s2 = v[:, 0:128] * v[:, 0:128]
        for k in range(1, 5):
            p = v[:, k * 128 : (k + 1) * 128]
            s1 = s1 + p
            s2 = s2 + p * p
        lanes = rows_at(b * 128, 128, 128)
        stat[w, 0:1, lanes] = jnp.sum(s1.T, 0, keepdims=True)
        stat[w, 1:2, lanes] = jnp.sum(s2.T, 0, keepdims=True)

    pl.semaphore_wait(bar, 17)

    st_cp = [send(stat.at[w], stat.at[w], st_s.at[d - 1], st_r.at[d - 1], at_w(d)) for d in range(1, 8)]
    for cp in st_cp:
        cp.start()

    loads["cot"].wait()

    @pl.loop(0, 9)
    def _(b):
        lanes = rows_at(b * 128, 128, 128)
        ids = jnp.broadcast_to(seg[lanes].reshape(1, 128), (R, 128))
        one = (ids == lax.broadcasted_iota(jnp.int32, (R, 128), 0)).astype(F32)
        oht[:, lanes] = one.astype(BF16)
        three = jnp.concatenate([one, one, one], 0)
        oh[lanes, :] = three.T.astype(BF16)
        gate = dot(oh[lanes, :], rmod[2])
        dout[lanes, :] = (cot[lanes, :].astype(F32) * gate).astype(BF16)

    def pair_sum(a, left, right):
        @pl.loop(0, NB)
        def _(b):
            p = dot(left[rows_at(b * BLK + (1 - c) * HALF, HALF), :], right[...], ((1,), (1,))).astype(BF16)
            for k in range(4):
                psib[a, b, k] = p[k * OWN : (k + 1) * OWN]

        cx = send(psib.at[a], rsib.at[a], cx_s.at[a], cx_r.at[a], sib)
        cx.start()

        @pl.loop(0, NB)
        def _(b):
            p = dot(left[rows_at(b * BLK + c * HALF, HALF), :], right[...], ((1,), (1,)))
            for k in range(4):
                pown[b, k] = p[k * OWN : (k + 1) * OWN]

        cx.wait()

        @pl.loop(0, NB)
        def _(b):
            for k in range(4):
                ysum[a, k, b] = (pown[b, k] + rsib[a, b, k].astype(F32)).astype(BF16)

    loads["wdn"].wait()
    pair_sum(0, dout, wdn)
    yd = []
    for d in (2, 1, 3):
        yd.append(send(ysum.at[0, (y + d) % 4], yrec.at[0, d - 1], yd_s.at[d - 1], yd_r.at[d - 1], at_y(d)))
        yd[-1].start()

    for cp in st_cp:
        cp.wait()
    tot = stat[0]
    for k in range(1, 8):
        tot = tot + stat[k]
    mu = tot[0:1] / D
    inv = lax.rsqrt(tot[1:2] / D - mu * mu + 1e-06)
    mu8 = jnp.broadcast_to(mu, (8, T))
    inv8 = jnp.broadcast_to(inv, (8, T))
    for b in range(9):
        lanes = slice(b * 128, (b + 1) * 128)
        col[0, lanes, :] = mu8[:, lanes].T
        col[1, lanes, :] = inv8[:, lanes].T

    @pl.loop(0, 9)
    def _(b):
        rows = rows_at(b * 128, 128, 128)
        shift = dot(oh[rows, :], rmod[0])
        gain = 1.0 + dot(oh[rows, :], rmod[1])
        xh = (tok[rows, :].astype(F32) - col[0, rows, 0:1]) * col[1, rows, 0:1]
        nrm[rows, :] = (xh * gain + shift).astype(BF16)

    loads["wup"].wait()
    pair_sum(1, nrm, wup)
    yu = {}
    for b in range(NB):
        for d in (2, 1, 3):
            yu[b, d] = send(
                ysum.at[1, (y + d) % 4, b], yrec.at[1, d - 1, b], yu_s.at[b, d - 1], yu_r.at[b, d - 1], at_y(d)
            )
            yu[b, d].start()
    for cp in yd:
        cp.wait()

    def total(a, b):
        v = ysum[a, y, b].astype(F32)
        for d in range(3):
            v = v + yrec[a, d, b].astype(F32)
        return v

    def own(kind, b, k, q):
        return had.at[kind, b, rows_at(k * HALF + q * OWN, OWN), :]

    ya, fw = {}, {}
    for b in range(NB):
        for d in (1, 2, 3):
            yu[b, d].wait()
        pre = total(1, b) + bias[...]
        sq = pre * pre
        th = jnp.tanh(ROOT * (pre + CUBE * (sq * pre)))
        slope = 0.5 * (1.0 + th) + (0.5 * ROOT) * pre * (1.0 - th * th) * (1.0 + (3.0 * CUBE) * sq)
        mine = rows_at(me * OWN, OWN)
        had[1, b, mine, :] = (total(0, b) * slope).astype(BF16)
        had[0, b, mine, :] = (0.5 * pre * (1.0 + th)).astype(BF16)
        src = own(1, b, c, y)
        for d in (2, 1, 3):
            ya[b, d] = send(src, src, ya_s.at[b, d - 1], ya_r.at[b, d - 1], at_y(d))
            ya[b, d].start()
        fw[b, 0] = send(src, src, fw_s.at[b, 0], fw_r.at[b, 0], sib)
        fw[b, 0].start()

    def own3(k, q):
        return had.at[0, :, rows_at(k * HALF + q * OWN, OWN), :]

    ha, hf = {}, {}
    for d in (2, 1, 3):
        ha[d] = send(own3(c, y), own3(c, y), ha_s.at[d - 1], ha_r.at[d - 1], at_y(d))
        ha[d].start()
    hf[0] = send(own3(c, y), own3(c, y), hf_s.at[0], hf_r.at[0], sib)
    hf[0].start()

    def zrow(b, d):
        return rows_at(b * BLK + ((z + d) % 8) * OWN, OWN)

    def gather(b):
        for d in (1, 3, 2):
            ya[b, d].wait()
            src = own(1, b, c, (y + 4 - d) % 4)
            fw[b, d] = send(src, src, fw_s.at[b, d], fw_r.at[b, d], sib)
            fw[b, d].start()
        for d in range(4):
            fw[b, d].wait()
        dn[b * BLK : (b + 1) * BLK, :] = dot(had[1, b], wup[...])

    zr = {}

    def hop(b, s):
        if s == 0:
            far = dn[zrow(b, 4), :].astype(BF16)
            sb[b, 0, 0, :, 0:CUT] = far[:, 0:CUT]
            sb[b, 1, 0, :, CUT:DW] = far[:, CUT:DW]
        else:
            for cp in zr[b, s - 1]:
                cp.wait()
            if s == 1:
                sb[b, 0, 1, :, 0:CUT] = (dn[zrow(b, 3), 0:CUT] + rb[b, 0, 0, :, 0:CUT].astype(F32)).astype(BF16)
                sb[b, 0, 1, :, CUT:DW] = dn[zrow(b, 3), CUT:DW].astype(BF16)
                sb[b, 1, 1, :, 0:CUT] = dn[zrow(b, 5), 0:CUT].astype(BF16)
                sb[b, 1, 1, :, CUT:DW] = (dn[zrow(b, 5), CUT:DW] + rb[b, 1, 0, :, CUT:DW].astype(F32)).astype(BF16)
            else:
                sb[b, 0, s] = (dn[zrow(b, 4 - s), :] + rb[b, 0, s - 1].astype(F32)).astype(BF16)
                sb[b, 1, s] = (dn[zrow(b, 4 + s), :] + rb[b, 1, s - 1].astype(F32)).astype(BF16)
        zr[b, s] = []
        for k, to in ((0, 1), (1, 7)):
            lanes = pl.ds(0, DW)
            if s == 0:
                lanes = pl.ds(k * CUT, CUT if k == 0 else DW - CUT)
            cp = send(
                sb.at[b, k, s, :, lanes], rb.at[b, k, s, :, lanes], zr_s.at[b, k, s], zr_r.at[b, k, s], at_z(to)
            )
            cp.start()
            zr[b, s].append(cp)

    def reach(b):
        return send(
            xs.at[b], xr.at[(x + 3 - b) % 4], xe_s.at[b], xe_r.at[(x + 3 - b) % 4], (w, z * 4 + b)
        )

    def land(b):
        for cp in zr[b, 3]:
            cp.wait()
        v = dn[zrow(b, 0), :] + rb[b, 0, 3].astype(F32) + rb[b, 1, 3].astype(F32)

        @pl.when(x == b)
        def _():
            zsum[...] = v

        @pl.when(x != b)
        def _():
            xs[b] = v.astype(BF16)
            reach(b).start()

    def table_block(b, carry):
        rows = rows_at(b * 128, 128, 128)
        dv = dn[rows, :]
        xh = (tok[rows, :].astype(F32) - col[0, rows, 0:1]) * col[1, rows, 0:1]
        hid = had[0, b // 3, rows_at((b % 3) * 128, 128, 128), :]
        yv = dot(hid, wdn[...]) * cot[rows, :].astype(F32)
        hot = oht[:, rows]
        out = []
        for acc, v in zip(carry, (dv, dv * xh, yv)):
            hi = v.astype(BF16)
            lo = (v - hi.astype(F32)).astype(BF16)
            out.append(acc + dot(hot, hi) + dot(hot, lo))
        return tuple(out)

    gather(0)
    hop(0, 0)
    gather(1)
    hop(1, 0)
    hop(0, 1)
    gather(2)
    hop(2, 0)
    hop(1, 1)
    hop(0, 2)
    for d in (1, 3, 2):
        ha[d].wait()
        src = own3(c, (y + 4 - d) % 4)
        hf[d] = send(src, src, hf_s.at[d], hf_r.at[d], sib)
        hf[d].start()
    hop(2, 1)
    hop(1, 2)
    hop(0, 3)
    for d in range(4):
        hf[d].wait()
    zero = jnp.zeros((R, DW), F32)
    sums = lax.fori_loop(0, 3, table_block, (zero, zero, zero))
    hop(2, 2)
    hop(1, 3)
    land(0)
    sums = lax.fori_loop(3, 6, table_block, sums)
    hop(2, 3)
    land(1)
    sums = lax.fori_loop(6, 9, table_block, sums)

    for k in range(3):
        for q in range(8):
            tx[k, 3, q] = sums[k][2 * q : 2 * q + 2]

    def kind_out(k):
        return send(
            tx.at[k, 3], tx.at[k, (x + 3 - k) % 4], tx_s.at[k], tx_r.at[(x + 3 - k) % 4], (w, z * 4 + k)
        )

    for k in range(3):
        @pl.when(x != k)
        def _():
            kind_out(k).start()

    def modul(b):
        rows = zrow(b, 0)
        gain = 1.0 + dot(oh[rows, :], rmod[1])
        rstd = col[1, rows, 0:1]
        xh = (tok[rows, :].astype(F32) - col[0, rows, 0:1]) * rstd
        return rows, gain, rstd, xh

    def ms_copies():
        return [send(mst.at[w], mst.at[w], ms_s.at[d - 1], ms_r.at[d - 1], at_w(d)) for d in range(1, 8)]

    def finish_sums(b):
        @pl.when(x == b)
        def _():
            for d in range(3):
                send(xs.at[0], xr.at[d], xe_s.at[0], xe_r.at[d], at_x(1)).wait_recv()
            v = zsum[...]
            for d in range(3):
                v = v + xr[d].astype(F32)
            rows, gain, rstd, xh = modul(b)
            dh = v * gain
            dhv[...] = dh
            dhx = dh * xh
            s1 = dh[:, 0:128]
            s2 = dhx[:, 0:128]
            for k in range(1, 5):
                s1 = s1 + dh[:, k * 128 : (k + 1) * 128]
                s2 = s2 + dhx[:, k * 128 : (k + 1) * 128]
            both = jnp.concatenate([s1, s2, jnp.zeros((128 - 2 * OWN, 128), F32)], 0)
            mst[w] = jnp.sum(both.T, 0, keepdims=True)
            for cp in ms_copies():
                cp.start()

    def give(b, d):
        rows = zrow(b, 0)
        return send(gx.at[rows], gx.at[rows], xg_s.at[d - 1], xg_r.at[b], at_x(d))

    def finish_rows(b):
        @pl.when(x == b)
        def _():
            for cp in ms_copies():
                cp.wait()
            m = mst[0]
            for k in range(1, 8):
                m = m + mst[k]
            mt = jnp.broadcast_to(m / D, (8, 128)).T
            rows, _, rstd, xh = modul(b)
            grad = cot[rows, :].astype(F32) + rstd * (dhv[...] - mt[0:OWN, 0:1] - xh * mt[OWN : 2 * OWN, 0:1])
            gx[rows, :] = grad.astype(BF16)
            for d in (2, 1, 3):
                give(b, d).start()

    finish_sums(0)
    land(2)
    finish_sums(1)
    finish_rows(0)
    finish_sums(2)
    finish_rows(1)
    finish_rows(2)

    zg = {}

    def spread(b, s):
        if s == 0:
            @pl.when(x != b)
            def _():
                give(b, 1).wait_recv()
        else:
            for cp in zg[b, s - 1]:
                cp.wait()
        if s < 4:
            zg[b, s] = []
            for k, (to, src) in enumerate(((1, 8 - s), (7, s))):
                lanes = pl.ds(0, DW)
                if s == 3:
                    lanes = pl.ds(k * CUT, CUT if k == 0 else DW - CUT)
                ref = gx.at[zrow(b, src), lanes]
                cp = send(ref, ref, zg_s.at[b, k, s], zg_r.at[b, k, s], at_z(to))
                cp.start()
                zg[b, s].append(cp)

    spread(0, 0)
    spread(1, 0)

    @pl.when(x < 3)
    def _():
        for d in range(3):
            send(tx.at[0, 3], tx.at[0, d], tx_s.at[0], tx_r.at[d], at_x(1)).wait_recv()
        tz[8] = (tx[x, 0] + tx[x, 1]) + (tx[x, 2] + tx[x, 3])
        for d in range(1, 8):
            send(tz.at[8, (z + d) % 8], tz.at[z, 0], tz_s.at[d - 1], tz_r.at[d - 1], at_z(d)).start()

    spread(0, 1)
    spread(2, 0)

    @pl.when(x < 3)
    def _():
        for d in range(1, 8):
            send(tz.at[8, 0], tz.at[0, 0], tz_s.at[d - 1], tz_r.at[d - 1], at_z(d)).wait()
        tz[z, 0] = tz[8, z]
        v = tz[0, 0]
        for k in range(1, 8):
            v = v + tz[k, 0]
        tf[x, z] = v
        for d in range(1, 8):
            send(tf.at[x, z], tf.at[x, z], tg_s.at[d - 1], tg_r.at[d - 1], at_z(d)).start()

    spread(1, 1)
    spread(0, 2)
    spread(2, 1)

    @pl.when(x < 3)
    def _():
        for d in range(1, 8):
            send(tf.at[x, z], tf.at[x, z], tg_s.at[d - 1], tg_r.at[d - 1], at_z(d)).wait()
        for d in range(1, 4):
            send(tf.at[x], tf.at[x], tb_s.at[d - 1], tb_r.at[x], at_x(d)).start()

    spread(1, 2)
    spread(0, 3)

    hid = had[0].reshape(T, FW)
    for m in range(4):
        n = min(128, FW - m * 128)
        gdn[m * 128 : m * 128 + n, :] = dot(hid[:, m * 128 : m * 128 + n], dout[...], ((0,), (0,)))
    out0 = pltpu.make_async_copy(gdn, gdn_h, out_s.at[0])
    out0.start()
    spread(2, 2)
    spread(1, 3)
    pre_g = had[1].reshape(T, FW)
    for m in range(4):
        n = min(128, FW - m * 128)
        gup[m * 128 : m * 128 + n, :] = dot(pre_g[:, m * 128 : m * 128 + n], nrm[...], ((0,), (0,)))
    out1 = pltpu.make_async_copy(gup, gup_h, out_s.at[1])
    out1.start()
    gb[...] = dot(jnp.ones((8, T), BF16), pre_g)[0:1]
    spread(2, 3)

    for k in range(3):
        @pl.when(x != k)
        def _():
            send(tf.at[k], tf.at[k], tb_s.at[0], tb_r.at[k], at_x(1)).wait_recv()
            kind_out(k).wait_send()
            reach(k).wait_send()

        @pl.when(x == k)
        def _():
            for d in range(1, 4):
                send(tf.at[k], tf.at[k], tb_s.at[d - 1], tb_r.at[k], at_x(d)).wait_send()
                give(k, d).wait_send()

    for k in range(3):
        for q in range(8):
            comp[k, 2 * q : 2 * q + 2, :] = tf[k, q]
        out = jnp.zeros((NS, DW), F32)
        for p in split3(comp[k]):
            out = out + dot(step_of, p, ((0,), (0,)))
        gtab[k] = out

    for b in range(NB):
        spread(b, 4)
    out0.wait()
    out1.wait()


def per_device(tokens, cotangent, w_up, bias_up, w_down, mod_table, seg_ids, step_ids):
    vm = pl.BlockSpec(memory_space=pltpu.VMEM)
    sm = pl.BlockSpec(memory_space=pltpu.SMEM)
    hbm = pl.BlockSpec(memory_space=pl.ANY)
    dma = pltpu.SemaphoreType.DMA
    outs = pl.pallas_call(
        kernel,
        out_shape=(
            jax.ShapeDtypeStruct((T, DW), BF16),
            jax.ShapeDtypeStruct((FW, DW), F32),
            jax.ShapeDtypeStruct((FW, DW), F32),
            jax.ShapeDtypeStruct((1, FW), F32),
            jax.ShapeDtypeStruct((3, NS, DW), F32),
        ),
        in_specs=[hbm, hbm, hbm, vm, hbm, vm, vm, sm],
        out_specs=(vm, hbm, hbm, vm, vm),
        scratch_shapes=[
            pltpu.VMEM((T, DW), BF16),
            pltpu.VMEM((T, DW), BF16),
            pltpu.VMEM((FW, DW), BF16),
            pltpu.VMEM((FW, DW), BF16),
            pltpu.VMEM((FW, DW), F32),
            pltpu.VMEM((FW, DW), F32),
            pltpu.VMEM((8, 2, T), F32),
            pltpu.VMEM((3, 3 * R, DW), BF16),
            pltpu.VMEM((T, 3 * R), BF16),
            pltpu.VMEM((R, T), BF16),
            pltpu.VMEM((2, T, 8), F32),
            pltpu.VMEM((T, DW), BF16),
            pltpu.VMEM((T, DW), BF16),
            pltpu.VMEM((2, NB, 4, OWN, FW), BF16),
            pltpu.VMEM((2, NB, 4, OWN, FW), BF16),
            pltpu.VMEM((NB, 4, OWN, FW), F32),
            pltpu.VMEM((2, 4, NB, OWN, FW), BF16),
            pltpu.VMEM((2, 3, NB, OWN, FW), BF16),
            pltpu.VMEM((2, NB, BLK, FW), BF16),
            pltpu.VMEM((T, DW), F32),
            pltpu.VMEM((NB, 2, 4, OWN, DW), BF16),
            pltpu.VMEM((NB, 2, 4, OWN, DW), BF16),
            pltpu.VMEM((OWN, DW), F32),
            pltpu.VMEM((NB, OWN, DW), BF16),
            pltpu.VMEM((3, OWN, DW), BF16),
            pltpu.VMEM((OWN, DW), F32),
            pltpu.VMEM((8, 1, 128), F32),
            pltpu.VMEM((3, 4, 8, 2, DW), F32),
            pltpu.VMEM((9, 8, 2, DW), F32),
            pltpu.VMEM((3, 8, 2, DW), F32),
            pltpu.VMEM((3, R, DW), F32),
            dma((4,)), dma((2,)),
            dma((7,)), dma((7,)),
            dma((2,)), dma((2,)),
            dma((3,)), dma((3,)),
            dma((NB, 3)), dma((NB, 3)),
            dma((NB, 3)), dma((NB, 3)),
            dma((NB, 4)), dma((NB, 4)),
            dma((3,)), dma((3,)),
            dma((4,)), dma((4,)),
            dma((NB, 2, 4)), dma((NB, 2, 4)),
            dma((NB,)), dma((3,)),
            dma((7,)), dma((7,)),
            dma((3,)), dma((NB,)),
            dma((NB, 2, 4)), dma((NB, 2, 4)),
            dma((3,)), dma((3,)),
            dma((7,)), dma((7,)),
            dma((7,)), dma((7,)),
            dma((3,)), dma((3,)),
        ],
        compiler_params=pltpu.CompilerParams(
            collective_id=0, has_side_effects=True, vmem_limit_bytes=56 * 1024 * 1024
        ),
        name="mlp_backward",
    )(
        tokens, cotangent, w_up.T, bias_up[None, :], w_down, mod_table.transpose(1, 0, 2), seg_ids, step_ids
    )
    return outs[0], outs[1].T, outs[2], outs[3][0], outs[4].transpose(1, 0, 2)


def solution(mesh):
    placed = (
        P(None, "width"),
        P(None, "width"),
        P("width", "hidden"),
        P("hidden"),
        P("hidden", "width"),
        P(None, None, "width"),
        P(),
        P(),
    )
    return jax.shard_map(
        per_device,
        mesh=mesh,
        in_specs=placed,
        out_specs=(
            P(None, "width"),
            P("width", "hidden"),
            P("hidden", "width"),
            P("hidden"),
            P(None, None, "width"),
        ),
        check_vma=False,
    )
```

```python
import functools

import jax
import jax.numpy as jnp
from jax import lax
from jax.experimental import pallas as pl
from jax.experimental.pallas import tpu as pltpu
from jax.sharding import PartitionSpec as P

MESH = pl.DeviceIdType.MESH
F32, BF16 = jnp.float32, jnp.bfloat16

T, DW, FW, R, NS = 1152, 640, 432, 16, 32
D = 5120
UNITS = (3, 3, 3)
NB = len(UNITS)
OB = tuple(16 * u for u in UNITS)
OFF = tuple(sum(OB[:b]) for b in range(NB))
CH = sum(OB)
CUT = 384
YCUT = 256
ROOT = 0.7978845608028654
CUBE = 0.044715


def split3(v):
    hi = v.astype(BF16)
    rest = v - hi.astype(F32)
    mid = rest.astype(BF16)
    return hi, mid, (rest - mid.astype(F32)).astype(BF16)


def dot(a, b, dims=((1,), (0,))):
    return lax.dot_general(a, b, (dims, ((), ())), preferred_element_type=F32)


def rows_at(start, size, step=16):
    return pl.ds(pl.multiple_of(start, step), size)


def kernel(
    tok_h, cot_h, wup_h, bias_h, wdn_h, tab_h, seg_h, stp,
    gx, gup, gdn, gb, gtab,
    tok, cot, wup, bias, wdn, tab, seg,
    stat, rmod, oh, oht, col, dout, nrm,
    psib, rsib, pown, yo, yh, ys, yr, had,
    dn, sb, rb, xa, dhv, mst,
    tx, tz, tf, comp,
    in_s, st_s, st_r, cx_s, cx_r, y_s, yh_r, yr_r, ag_s, a1_r, a2_r, fw_r,
    zr_s, zr_r, xe_s, xe_r, ms_s, ms_r, zg_s, zg_r,
    tx_s, tx_r, tz_s, tz_r, tg_s, tg_r, tb_s, tb_r,
):
    w = lax.axis_index("width")
    h = lax.axis_index("hidden")
    y, c = w // 2, w % 2
    z, x = h // 4, h % 4

    def at_w(d):
        return ((w + d) % 8, h)

    def at_y(d):
        return (((y + d) % 4) * 2 + c, h)

    sib = (y * 2 + 1 - c, h)

    def at_z(d):
        return (w, ((z + d) % 8) * 4 + x)

    def at_x(d):
        return (w, z * 4 + (x + d) % 4)

    def send(src, dst, s_sem, r_sem, dev):
        return pltpu.make_async_remote_copy(
            src_ref=src, dst_ref=dst, send_sem=s_sem, recv_sem=r_sem, device_id=dev, device_id_type=MESH
        )

    def received(ref, sem):
        send(ref, ref, sem, sem, sib).wait_recv()

    def sent(ref, sem):
        send(ref, ref, sem, sem, sib).wait_send()

    loads = {}
    for i, (name, src, dst) in enumerate(
        (
            ("tok", tok_h, tok), ("tab", tab_h, tab), ("seg", seg_h, seg), ("cot", cot_h, cot),
            ("wdn", wdn_h, wdn), ("wup", wup_h, wup), ("bias", bias_h, bias),
        )
    ):
        loads[name] = pltpu.make_async_copy(src, dst, in_s.at[i])
        loads[name].start()

    bar = pltpu.get_barrier_semaphore()
    for d in range(1, 8):
        pl.semaphore_signal(bar, inc=1, device_id=at_w(d), device_id_type=MESH)
        pl.semaphore_signal(bar, inc=1, device_id=at_z(d), device_id_type=MESH)
    for d in range(1, 4):
        pl.semaphore_signal(bar, inc=1, device_id=at_x(d), device_id_type=MESH)

    loads["tok"].wait()

    @pl.loop(0, 9)
    def _(b):
        v = tok[rows_at(b * 128, 128, 128), :].astype(F32)
        s1 = v[:, 0:128]
        s2 = v[:, 0:128] * v[:, 0:128]
        for k in range(1, 5):
            p = v[:, k * 128 : (k + 1) * 128]
            s1 = s1 + p
            s2 = s2 + p * p
        lanes = rows_at(b * 128, 128, 128)
        stat[w, 0:1, lanes] = jnp.sum(s1.T, 0, keepdims=True)
        stat[w, 1:2, lanes] = jnp.sum(s2.T, 0, keepdims=True)

    row = lax.broadcasted_iota(jnp.int32, (R, NS), 0)
    picked = jnp.zeros((R, NS), jnp.int32)
    for r in range(R):
        picked = jnp.where(row == r, stp[r], picked)
    step_of = (picked == lax.broadcasted_iota(jnp.int32, (R, NS), 1)).astype(F32).astype(BF16)
    loads["tab"].wait()
    for k in range(3):
        parts = split3(tab[k])
        rm = dot(step_of, parts[0]) + dot(step_of, parts[1]) + dot(step_of, parts[2])
        for i, piece in enumerate(split3(rm)):
            rmod[k, i * R : (i + 1) * R, :] = piece

    pl.semaphore_wait(bar, 17)
    for d in range(1, 8):
        send(stat.at[w], stat.at[w], st_s.at[0], st_r.at[0], at_w(d)).start()

    loads["seg"].wait()
    loads["cot"].wait()

    @pl.loop(0, 9)
    def _(b):
        lanes = rows_at(b * 128, 128, 128)
        ids = jnp.broadcast_to(seg[lanes].reshape(1, 128), (R, 128))
        one = (ids == lax.broadcasted_iota(jnp.int32, (R, 128), 0)).astype(F32)
        oht[:, lanes] = one.astype(BF16)
        three = jnp.concatenate([one, one, one], 0)
        oh[lanes, :] = three.T.astype(BF16)
        gate = dot(oh[lanes, :], rmod[2])
        dout[lanes, :] = (cot[lanes, :].astype(F32) * gate).astype(BF16)

    def base(b, k):
        return 8 * OFF[b] + k * 4 * OB[b]

    def part(b):
        return slice(OFF[b], OFF[b] + OB[b])

    def four(b):
        return slice(4 * OFF[b], 4 * OFF[b] + 4 * OB[b])

    def target(b, d):
        return rows_at(4 * OFF[b] + ((y + d) % 4) * OB[b], OB[b])

    LO, HI = slice(0, YCUT), slice(YCUT, FW)
    cx = {}

    def to_core(a, b, left, right):
        psib[a, four(b)] = dot(left[rows_at(base(b, 1 - c), 4 * OB[b]), :], right[...], ((1,), (1,))).astype(BF16)
        cx[a, b] = send(psib.at[a, four(b)], rsib.at[a, four(b)], cx_s.at[a, b], cx_r.at[a, b], sib)
        cx[a, b].start()

    def to_opposite(a, b, left, right):
        p = dot(left[rows_at(base(b, c), 4 * OB[b]), :], right[...], ((1,), (1,)))
        cx[a, b].wait()
        pown[a, four(b)] = p + rsib[a, four(b)].astype(F32)
        yo[a, part(b)] = pown[a, target(b, 2), :].astype(BF16)
        for lanes, k, d in ((LO, 0, 1), (HI, 1, 3)):
            send(
                yo.at[a, part(b), lanes], yh.at[a, part(b), lanes], y_s.at[a, b], yh_r.at[a, b, k], at_y(d)
            ).start()

    def to_neighbours(a, b):
        for lanes, rest, k, d in ((LO, HI, 0, 1), (HI, LO, 1, 3)):
            received(yh.at[a, part(b), lanes], yh_r.at[a, b, k])
            mine = pown[a, target(b, d), :]
            ys[a, k, part(b), lanes] = (mine[:, lanes] + yh[a, part(b), lanes].astype(F32)).astype(BF16)
            ys[a, k, part(b), rest] = mine[:, rest].astype(BF16)
            send(
                ys.at[a, k, part(b)], yr.at[a, k, part(b)], y_s.at[a, b], yr_r.at[a, b, k], at_y(d)
            ).start()

    loads["wdn"].wait()
    for b in range(NB):
        to_core(0, b, dout, wdn)
    for b in range(NB):
        to_opposite(0, b, dout, wdn)

    received(stat.at[0:7], st_r.at[0])
    tot = stat[0]
    for k in range(1, 8):
        tot = tot + stat[k]
    mu = tot[0:1] / D
    inv = lax.rsqrt(tot[1:2] / D - mu * mu + 1e-06)
    mu8 = jnp.broadcast_to(mu, (8, T))
    inv8 = jnp.broadcast_to(inv, (8, T))
    for b in range(9):
        lanes = slice(b * 128, (b + 1) * 128)
        col[0, lanes, :] = mu8[:, lanes].T
        col[1, lanes, :] = inv8[:, lanes].T

    def normalize(first, last):
        @pl.loop(first, last)
        def _(b):
            rows = rows_at(b * 128, 128, 128)
            shift = dot(oh[rows, :], rmod[0])
            gain = 1.0 + dot(oh[rows, :], rmod[1])
            xh = (tok[rows, :].astype(F32) - col[0, rows, 0:1]) * col[1, rows, 0:1]
            nrm[rows, :] = (xh * gain + shift).astype(BF16)

    loads["wup"].wait()
    loads["bias"].wait()
    unit = 0
    for b in range(NB):
        normalize(unit, unit + UNITS[b])
        unit += UNITS[b]
        to_core(1, b, nrm, wup)
        to_neighbours(0, b)
    for b in range(NB):
        to_opposite(1, b, nrm, wup)

    def total(a, b):
        v = pown[a, target(b, 0), :]
        for k in range(2):
            v = v + yr[a, k, part(b)].astype(F32)
        return v

    def chunk(b, k, d):
        return rows_at(base(b, k) + ((y + d) % 4) * OB[b], OB[b])

    def activate(b):
        for a in range(2):
            for k in range(2):
                received(yr.at[a, k, part(b)], yr_r.at[a, b, k])
        pre = total(1, b) + bias[...]
        sq = pre * pre
        th = jnp.tanh(ROOT * (pre + CUBE * (sq * pre)))
        slope = 0.5 * (1.0 + th) + (0.5 * ROOT) * pre * (1.0 - th * th) * (1.0 + (3.0 * CUBE) * sq)
        had[1, chunk(b, c, 0), :] = (total(0, b) * slope).astype(BF16)
        had[0, chunk(b, c, 0), :] = (0.5 * pre * (1.0 + th)).astype(BF16)

    def pass_on(g, b, d, lanes, r_sem, dev):
        ref = had.at[g, chunk(b, c, d), lanes]
        send(ref, ref, ag_s.at[g, b], r_sem, dev).start()

    ALL = slice(0, FW)

    def spread_first(g, b):
        pass_on(g, b, 0, ALL, a1_r.at[g, b, 0], at_y(1))
        pass_on(g, b, 0, ALL, a1_r.at[g, b, 1], at_y(3))
        pass_on(g, b, 0, ALL, fw_r.at[g, b], sib)

    def spread_second(g, b):
        for k, d, to, lanes in ((0, 3, 1, LO), (1, 1, 3, HI)):
            received(had.at[g, chunk(b, c, d), :], a1_r.at[g, b, k])
            pass_on(g, b, d, lanes, a2_r.at[g, b, k], at_y(to))
            pass_on(g, b, d, ALL, fw_r.at[g, b], sib)

    def spread_third(g, b):
        for k, lanes in ((0, LO), (1, HI)):
            received(had.at[g, chunk(b, c, 2), lanes], a2_r.at[g, b, k])
        pass_on(g, b, 2, ALL, fw_r.at[g, b], sib)

    def spread_done(g, b):
        received(had.at[g, rows_at(base(b, 1 - c), 4 * OB[b]), :], fw_r.at[g, b])

    def zrow(b, d):
        return rows_at(8 * OFF[b] + ((z + d) % 8) * OB[b], OB[b])

    def norm_part(b):
        block = slice(8 * OFF[b], 8 * (OFF[b] + OB[b]))
        dn[block, :] = dot(had[1, block], wup[...])

    def zlanes(k, half):
        if not half:
            return slice(0, DW)
        return slice(0, CUT) if k == 0 else slice(CUT, DW)

    def hop(b, s):
        n = OB[b]
        for k, sign, to in ((0, -1, 1), (1, 1, 7)):
            mine = dn[zrow(b, 4 + sign * s), :]
            lanes = zlanes(k, s == 0)
            slot = k * 4 + s
            if s > 0:
                came = zlanes(k, s == 1)
                received(rb.at[b, slot - 1, 0:n, came], zr_r.at[b, slot - 1])
                if s == 1:
                    rest = zlanes(1 - k, True)
                    sb[b, slot, 0:n, rest] = mine[:, rest].astype(BF16)
                sb[b, slot, 0:n, came] = (mine[:, came] + rb[b, slot - 1, 0:n, came].astype(F32)).astype(BF16)
            else:
                sb[b, slot, 0:n, lanes] = mine[:, lanes].astype(BF16)
            send(
                sb.at[b, slot, 0:n, lanes], rb.at[b, slot, 0:n, lanes], zr_s.at[b], zr_r.at[b, slot], at_z(to)
            ).start()

    def land(b):
        n = OB[b]
        v = dn[zrow(b, 0), :]
        for k in range(2):
            received(rb.at[b, 4 * k + 3, 0:n], zr_r.at[b, 4 * k + 3])
            v = v + rb[b, 4 * k + 3, 0:n].astype(F32)
        xa[b, x, 0:n] = v.astype(BF16)
        ref = xa.at[b, x, 0:n]
        for d in (2, 1, 3):
            send(ref, ref, xe_s.at[b], xe_r.at[b], at_x(d)).start()

    def modul(b):
        rows = zrow(b, 0)
        gain = 1.0 + dot(oh[rows, :], rmod[1])
        rstd = col[1, rows, 0:1]
        xh = (tok[rows, :].astype(F32) - col[0, rows, 0:1]) * rstd
        return rows, gain, rstd, xh

    def finish_sums(b):
        n = OB[b]
        received(xa.at[b, 0:3, 0:n], xe_r.at[b])
        v = [xa[b, k, 0:n].astype(F32) for k in range(4)]
        v = (v[0] + v[1]) + (v[2] + v[3])
        rows, gain, rstd, xh = modul(b)
        dh = v * gain
        dhv[b, 0:n] = dh
        dhx = dh * xh
        s1 = dh[:, 0:128]
        s2 = dhx[:, 0:128]
        for k in range(1, 5):
            s1 = s1 + dh[:, k * 128 : (k + 1) * 128]
            s2 = s2 + dhx[:, k * 128 : (k + 1) * 128]
        both = jnp.concatenate([s1, s2, jnp.zeros((128 - 2 * n, 128), F32)], 0)
        mst[b, w] = jnp.sum(both.T, 0, keepdims=True)
        ref = mst.at[b, w]
        for d in range(1, 8):
            send(ref, ref, ms_s.at[b], ms_r.at[b], at_w(d)).start()

    def finish_rows(b):
        received(mst.at[b, 0:7], ms_r.at[b])
        n = OB[b]
        m = mst[b, 0]
        for k in range(1, 8):
            m = m + mst[b, k]
        mt = jnp.broadcast_to(m / D, (8, 128)).T
        rows, _, rstd, xh = modul(b)
        grad = cot[rows, :].astype(F32) + rstd * (dhv[b, 0:n] - mt[0:n, 0:1] - xh * mt[n : 2 * n, 0:1])
        gx[rows, :] = grad.astype(BF16)

    def ring(b, s):
        for k, sign, to in ((0, -1, 1), (1, 1, 7)):
            if s > 0:
                received(gx.at[zrow(b, 8 + sign * s), zlanes(k, s == 4)], zg_r.at[b, k, s - 1])
            if s < 4:
                ref = gx.at[zrow(b, 8 + sign * s), zlanes(k, s == 3)]
                send(ref, ref, zg_s.at[b], zg_r.at[b, k, s], at_z(to)).start()

    def table_block(b, carry):
        rows = rows_at(b * 128, 128, 128)
        dv = dn[rows, :]
        xh = (tok[rows, :].astype(F32) - col[0, rows, 0:1]) * col[1, rows, 0:1]
        yv = dot(had[0, rows, :], wdn[...]) * cot[rows, :].astype(F32)
        hot = oht[:, rows]
        out = []
        for acc, v in zip(carry, (dv, dv * xh, yv)):
            hi = v.astype(BF16)
            lo = (v - hi.astype(F32)).astype(BF16)
            out.append(acc + dot(hot, hi) + dot(hot, lo))
        return tuple(out)

    def kind_out(k):
        return send(
            tx.at[k, 3], tx.at[k, (x + 3 - k) % 4], tx_s.at[k], tx_r.at[0], (w, z * 4 + k)
        )

    def weight_gradient(out, left, right):
        for m in range(4):
            n = min(128, FW - m * 128)
            out[m * 128 : m * 128 + n, :] = dot(left[:, m * 128 : m * 128 + n], right[...], ((0,), (0,)))

    to_neighbours(1, 0)
    to_neighbours(1, 1)
    activate(0)
    spread_first(1, 0)
    to_neighbours(1, 2)
    activate(1)
    spread_first(1, 1)
    spread_second(1, 0)
    activate(2)
    spread_first(1, 2)
    spread_second(1, 1)
    spread_third(1, 0)
    spread_done(1, 0)
    norm_part(0)
    hop(0, 0)
    spread_second(1, 2)
    spread_third(1, 1)
    for b in range(NB):
        spread_first(0, b)
    spread_done(1, 1)
    norm_part(1)
    hop(1, 0)
    hop(0, 1)
    spread_third(1, 2)
    spread_done(1, 2)
    norm_part(2)
    hop(2, 0)
    spread_second(0, 0)
    hop(1, 1)
    hop(0, 2)
    spread_second(0, 1)
    hop(2, 1)
    spread_second(0, 2)
    hop(1, 2)
    spread_third(0, 0)
    hop(0, 3)
    spread_third(0, 1)
    hop(2, 2)
    spread_third(0, 2)
    zero = jnp.zeros((R, DW), F32)
    spread_done(0, 0)
    sums = lax.fori_loop(0, 2, table_block, (zero, zero, zero))
    hop(1, 3)
    land(0)
    spread_done(0, 1)
    spread_done(0, 2)
    sums = lax.fori_loop(2, 4, table_block, sums)
    hop(2, 3)
    land(1)
    finish_sums(0)
    sums = lax.fori_loop(4, 6, table_block, sums)
    land(2)
    finish_rows(0)
    ring(0, 0)
    finish_sums(1)
    sums = lax.fori_loop(6, 9, table_block, sums)

    for k in range(3):
        for q in range(8):
            tx[k, 3, q] = sums[k][2 * q : 2 * q + 2]
    for k in range(3):
        @pl.when(x != k)
        def _():
            kind_out(k).start()

    finish_sums(2)
    finish_rows(1)
    ring(1, 0)
    ring(0, 1)
    finish_rows(2)
    ring(2, 0)
    ring(1, 1)
    ring(0, 2)

    @pl.when(x < 3)
    def _():
        received(tx.at[0, 0:3], tx_r.at[0])
        tz[8] = (tx[x, 0] + tx[x, 1]) + (tx[x, 2] + tx[x, 3])
        for d in range(1, 8):
            send(tz.at[8, (z + d) % 8], tz.at[z, 0], tz_s.at[0], tz_r.at[0], at_z(d)).start()

    weight_gradient(gdn, had[0], dout)
    ring(2, 1)
    ring(1, 2)
    ring(0, 3)

    @pl.when(x < 3)
    def _():
        received(tz.at[0:7, 0], tz_r.at[0])
        sent(tz.at[0:7, 0], tz_s.at[0])
        tz[z, 0] = tz[8, z]
        v = tz[0, 0]
        for k in range(1, 8):
            v = v + tz[k, 0]
        tf[x, z] = v
        for d in range(1, 8):
            send(tf.at[x, z], tf.at[x, z], tg_s.at[0], tg_r.at[0], at_z(d)).start()

    weight_gradient(gup, had[1], nrm)
    ring(2, 2)
    ring(1, 3)

    @pl.when(x < 3)
    def _():
        received(tf.at[x, 0:7], tg_r.at[0])
        sent(tf.at[x, 0:7], tg_s.at[0])
        for d in range(1, 4):
            send(tf.at[x], tf.at[x], tb_s.at[0], tb_r.at[x], at_x(d)).start()

    gb[...] = dot(jnp.ones((8, T), BF16), had[1])[0:1]
    ring(2, 3)
    sent(stat.at[0:7], st_s.at[0])
    for b in range(NB):
        n = OB[b]
        for a in range(2):
            sent(psib.at[a, 0 : 3 * n], y_s.at[a, b])
            sent(had.at[a, 0 : 7 * n], ag_s.at[a, b])
        sent(sb.at[b, 0:7, 0:n], zr_s.at[b])
        sent(xa.at[b, 0:3, 0:n], xe_s.at[b])
        sent(mst.at[b, 0:7], ms_s.at[b])

    for k in range(3):
        @pl.when(x != k)
        def _():
            received(tf.at[k], tb_r.at[k])
            kind_out(k).wait_send()

    @pl.when(x < 3)
    def _():
        sent(tf.at[0:3], tb_s.at[0])

    for k in range(3):
        for q in range(8):
            comp[k, 2 * q : 2 * q + 2, :] = tf[k, q]
        out = jnp.zeros((NS, DW), F32)
        for p in split3(comp[k]):
            out = out + dot(step_of, p, ((0,), (0,)))
        gtab[k] = out

    for b in range(NB):
        ring(b, 4)
        sent(gx.at[0 : 7 * OB[b]], zg_s.at[b])


def flush(*refs):
    copies = [pltpu.make_async_copy(refs[k], refs[5 + k], refs[10].at[k]) for k in range(5)]
    for cp in copies:
        cp.start()
    for cp in copies:
        cp.wait()


def per_device(tokens, cotangent, w_up, bias_up, w_down, mod_table, seg_ids, step_ids):
    vm = pl.BlockSpec(memory_space=pltpu.VMEM)
    sm = pl.BlockSpec(memory_space=pltpu.SMEM)
    hbm = pl.BlockSpec(memory_space=pltpu.HBM)
    dma = pltpu.SemaphoreType.DMA
    shapes = (
        jax.ShapeDtypeStruct((T, DW), BF16),
        jax.ShapeDtypeStruct((FW, DW), F32),
        jax.ShapeDtypeStruct((FW, DW), F32),
        jax.ShapeDtypeStruct((1, FW), F32),
        jax.ShapeDtypeStruct((3, NS, DW), F32),
    )
    outs = pl.pallas_call(
        kernel,
        out_shape=shapes,
        in_specs=[hbm] * 7 + [sm],
        out_specs=(vm,) * 5,
        scratch_shapes=[
            pltpu.VMEM((T, DW), BF16),
            pltpu.VMEM((T, DW), BF16),
            pltpu.VMEM((FW, DW), BF16),
            pltpu.VMEM((1, FW), F32),
            pltpu.VMEM((FW, DW), BF16),
            pltpu.VMEM((3, NS, DW), F32),
            pltpu.VMEM((T,), jnp.int32),
            pltpu.VMEM((8, 2, T), F32),
            pltpu.VMEM((3, 3 * R, DW), BF16),
            pltpu.VMEM((T, 3 * R), BF16),
            pltpu.VMEM((R, T), BF16),
            pltpu.VMEM((2, T, 8), F32),
            pltpu.VMEM((T, DW), BF16),
            pltpu.VMEM((T, DW), BF16),
            pltpu.VMEM((2, 4 * CH, FW), BF16),
            pltpu.VMEM((2, 4 * CH, FW), BF16),
            pltpu.VMEM((2, 4 * CH, FW), F32),
            pltpu.VMEM((2, CH, FW), BF16),
            pltpu.VMEM((2, CH, FW), BF16),
            pltpu.VMEM((2, 2, CH, FW), BF16),
            pltpu.VMEM((2, 2, CH, FW), BF16),
            pltpu.VMEM((2, T, FW), BF16),
            pltpu.VMEM((T, DW), F32),
            pltpu.VMEM((NB, 8, OB[0], DW), BF16),
            pltpu.VMEM((NB, 8, OB[0], DW), BF16),
            pltpu.VMEM((NB, 4, OB[0], DW), BF16),
            pltpu.VMEM((NB, OB[0], DW), F32),
            pltpu.VMEM((NB, 8, 1, 128), F32),
            pltpu.VMEM((3, 4, 8, 2, DW), F32),
            pltpu.VMEM((9, 8, 2, DW), F32),
            pltpu.VMEM((3, 8, 2, DW), F32),
            pltpu.VMEM((3, R, DW), F32),
            dma((7,)),
            dma((1,)), dma((1,)),
            dma((2, NB)), dma((2, NB)),
            dma((2, NB)), dma((2, NB, 2)), dma((2, NB, 2)),
            dma((2, NB)), dma((2, NB, 2)), dma((2, NB, 2)), dma((2, NB)),
            dma((NB,)), dma((NB, 8)),
            dma((NB,)), dma((NB,)),
            dma((NB,)), dma((NB,)),
            dma((NB,)), dma((NB, 2, 4)),
            dma((3,)), dma((1,)),
            dma((1,)), dma((1,)),
            dma((1,)), dma((1,)),
            dma((1,)), dma((3,)),
        ],
        compiler_params=pltpu.CompilerParams(
            collective_id=0, has_side_effects=True, vmem_limit_bytes=34 * 1024 * 1024
        ),
        name="mlp_backward",
    )(
        *(
            pltpu.with_memory_space_constraint(v, pltpu.HBM)
            for v in (tokens, cotangent, w_up.T, bias_up[None, :], w_down, mod_table.transpose(1, 0, 2), seg_ids)
        ),
        step_ids,
    )
    outs = pl.pallas_call(
        flush,
        out_shape=shapes,
        in_specs=[vm] * 5,
        out_specs=(hbm,) * 5,
        scratch_shapes=[dma((5,))],
        compiler_params=pltpu.CompilerParams(vmem_limit_bytes=1024 * 1024),
        name="write_out",
    )(*outs)
    return outs[0], outs[1].T, outs[2], outs[3][0], outs[4].transpose(1, 0, 2)


def solution(mesh):
    placed = (
        P(None, "width"),
        P(None, "width"),
        P("width", "hidden"),
        P("hidden"),
        P("hidden", "width"),
        P(None, None, "width"),
        P(),
        P(),
    )
    return jax.shard_map(
        per_device,
        mesh=mesh,
        in_specs=placed,
        out_specs=(
            P(None, "width"),
            P("width", "hidden"),
            P("hidden", "width"),
            P("hidden"),
            P(None, None, "width"),
        ),
        check_vma=False,
    )
```

```python
import functools

import jax
import jax.numpy as jnp
from jax import lax
from jax.experimental import pallas as pl
from jax.experimental.pallas import tpu as pltpu
from jax.sharding import PartitionSpec as P

MESH = pl.DeviceIdType.MESH
F32, BF16 = jnp.float32, jnp.bfloat16

T, DW, FW, R, NS = 1152, 640, 432, 16, 32
D = 5120
UNITS = (3, 3, 3)
NB = len(UNITS)
OB = tuple(16 * u for u in UNITS)
OFF = tuple(sum(OB[:b]) for b in range(NB))
CH = sum(OB)
CUT = 384
ROOT = 0.7978845608028654
CUBE = 0.044715


def split3(v):
    hi = v.astype(BF16)
    rest = v - hi.astype(F32)
    mid = rest.astype(BF16)
    return hi, mid, (rest - mid.astype(F32)).astype(BF16)


def dot(a, b, dims=((1,), (0,))):
    return lax.dot_general(a, b, (dims, ((), ())), preferred_element_type=F32)


def rows_at(start, size, step=16):
    return pl.ds(pl.multiple_of(start, step), size)


def kernel(
    tok_h, cot_h, wup_h, bias_h, wdn_h, tab_h, seg_h, stp_h,
    gx, gup, gdn, gb, gtab,
    tok, cot, wup, bias, wdn, tab, seg, stp,
    stat, rmod, oh, oht, col, dout, nrm,
    psib, rsib, pown, ys, yr, had,
    dn, sb, rb, xa, dhv, mst,
    tx, tz, tf, comp,
    in_s, st_s, st_r, cx_s, cx_r, y_s, yr_r, ag_s, a1_r, fw_r,
    zr_s, zr_r, xe_s, xe_r, ms_s, ms_r, zg_s, zg_r,
    tx_s, tx_r, tz_s, tz_r, tg_s, tg_r, tb_s, tb_r,
):
    w = lax.axis_index("width")
    h = lax.axis_index("hidden")
    y, c = w // 2, w % 2
    z, x = h // 4, h % 4

    def at_w(d):
        return ((w + d) % 8, h)

    def at_y(d):
        return (((y + d) % 4) * 2 + c, h)

    sib = (y * 2 + 1 - c, h)

    def at_z(d):
        return (w, ((z + d) % 8) * 4 + x)

    def at_x(d):
        return (w, z * 4 + (x + d) % 4)

    def send(src, dst, s_sem, r_sem, dev):
        return pltpu.make_async_remote_copy(
            src_ref=src, dst_ref=dst, send_sem=s_sem, recv_sem=r_sem, device_id=dev, device_id_type=MESH
        )

    def received(ref, sem):
        send(ref, ref, sem, sem, sib).wait_recv()

    def sent(ref, sem):
        send(ref, ref, sem, sem, sib).wait_send()

    loads = {}
    for i, (name, src, dst) in enumerate(
        (
            ("tok", tok_h, tok), ("stp", stp_h, stp), ("tab", tab_h, tab), ("seg", seg_h, seg), ("cot", cot_h, cot),
            ("wdn", wdn_h, wdn), ("wup", wup_h, wup), ("bias", bias_h, bias),
        )
    ):
        loads[name] = pltpu.make_async_copy(src, dst, in_s.at[i])
        loads[name].start()

    bar = pltpu.get_barrier_semaphore()
    for d in range(1, 8):
        pl.semaphore_signal(bar, inc=1, device_id=at_w(d), device_id_type=MESH)
        pl.semaphore_signal(bar, inc=1, device_id=at_z(d), device_id_type=MESH)
    for d in range(1, 4):
        pl.semaphore_signal(bar, inc=1, device_id=at_x(d), device_id_type=MESH)

    loads["tok"].wait()

    @pl.loop(0, 9)
    def _(b):
        v = tok[rows_at(b * 128, 128, 128), :].astype(F32)
        s1 = v[:, 0:128]
        s2 = v[:, 0:128] * v[:, 0:128]
        for k in range(1, 5):
            p = v[:, k * 128 : (k + 1) * 128]
            s1 = s1 + p
            s2 = s2 + p * p
        lanes = rows_at(b * 128, 128, 128)
        stat[w, 0:1, lanes] = jnp.sum(s1.T, 0, keepdims=True)
        stat[w, 1:2, lanes] = jnp.sum(s2.T, 0, keepdims=True)

    pl.semaphore_wait(bar, 17)
    for d in range(1, 8):
        send(stat.at[w], stat.at[w], st_s.at[0], st_r.at[0], at_w(d)).start()

    loads["stp"].wait()
    ids = jnp.broadcast_to(stp[...].reshape(1, R), (NS, R))
    step_of = (ids == lax.broadcasted_iota(jnp.int32, (NS, R), 0)).astype(F32).astype(BF16)
    loads["tab"].wait()
    for k in range(3):
        parts = split3(tab[k])
        rm = sum(dot(step_of, piece, ((0,), (0,))) for piece in parts)
        for i, piece in enumerate(split3(rm)):
            rmod[k, i * R : (i + 1) * R, :] = piece

    def units(b):
        return sum(UNITS[:b]), sum(UNITS[: b + 1])

    def outer(b):
        @pl.loop(*units(b))
        def _(i):
            lanes = rows_at(i * 128, 128, 128)
            ids = jnp.broadcast_to(seg[lanes].reshape(1, 128), (R, 128))
            one = (ids == lax.broadcasted_iota(jnp.int32, (R, 128), 0)).astype(F32)
            oht[:, lanes] = one.astype(BF16)
            three = jnp.concatenate([one, one, one], 0)
            oh[lanes, :] = three.T.astype(BF16)
            gate = dot(oh[lanes, :], rmod[2])
            dout[lanes, :] = (cot[lanes, :].astype(F32) * gate).astype(BF16)

    def base(b, k):
        return 8 * OFF[b] + k * 4 * OB[b]

    def part(b):
        return slice(OFF[b], OFF[b] + OB[b])

    def four(b):
        return slice(4 * OFF[b], 4 * OFF[b] + 4 * OB[b])

    def target(b, d):
        return rows_at(4 * OFF[b] + ((y + d) % 4) * OB[b], OB[b])

    cx = {}

    def to_core(a, b, left, right):
        psib[a, four(b)] = dot(left[rows_at(base(b, 1 - c), 4 * OB[b]), :], right[...], ((1,), (1,))).astype(BF16)
        cx[a, b] = send(psib.at[a, four(b)], rsib.at[a, four(b)], cx_s.at[a, b], cx_r.at[a, b], sib)
        cx[a, b].start()

    def to_chips(a, b, left, right):
        p = dot(left[rows_at(base(b, c), 4 * OB[b]), :], right[...], ((1,), (1,)))
        cx[a, b].wait()
        pown[a, four(b)] = p + rsib[a, four(b)].astype(F32)
        for d in (2, 1, 3):
            ys[a, d - 1, part(b)] = pown[a, target(b, d), :].astype(BF16)
            send(
                ys.at[a, d - 1, part(b)], yr.at[a, d - 1, part(b)], y_s.at[a, b], yr_r.at[a, b, d - 1], at_y(d)
            ).start()

    def columns():
        received(stat.at[0:7], st_r.at[0])
        tot = stat[0]
        for k in range(1, 8):
            tot = tot + stat[k]
        mu = tot[0:1] / D
        inv = lax.rsqrt(tot[1:2] / D - mu * mu + 1e-06)
        mu8 = jnp.broadcast_to(mu, (8, T))
        inv8 = jnp.broadcast_to(inv, (8, T))
        for b in range(9):
            lanes = slice(b * 128, (b + 1) * 128)
            col[0, lanes, :] = mu8[:, lanes].T
            col[1, lanes, :] = inv8[:, lanes].T

    def normalize(b):
        @pl.loop(*units(b))
        def _(i):
            rows = rows_at(i * 128, 128, 128)
            shift = dot(oh[rows, :], rmod[0])
            gain = 1.0 + dot(oh[rows, :], rmod[1])
            xh = (tok[rows, :].astype(F32) - col[0, rows, 0:1]) * col[1, rows, 0:1]
            nrm[rows, :] = (xh * gain + shift).astype(BF16)

    def total(a, b):
        v = pown[a, target(b, 0), :]
        for k in range(3):
            v = v + yr[a, k, part(b)].astype(F32)
        return v

    def chunk(b, k, d):
        return rows_at(base(b, k) + ((y + d) % 4) * OB[b], OB[b])

    def activate(b):
        for a in range(2):
            for k in range(3):
                received(yr.at[a, k, part(b)], yr_r.at[a, b, k])
        pre = total(1, b) + bias[...]
        sq = pre * pre
        th = jnp.tanh(ROOT * (pre + CUBE * (sq * pre)))
        slope = 0.5 * (1.0 + th) + (0.5 * ROOT) * pre * (1.0 - th * th) * (1.0 + (3.0 * CUBE) * sq)
        had[1, chunk(b, c, 0), :] = (total(0, b) * slope).astype(BF16)
        had[0, chunk(b, c, 0), :] = (0.5 * pre * (1.0 + th)).astype(BF16)

    def pass_on(g, b, d, r_sem, dev):
        ref = had.at[g, chunk(b, c, d), :]
        send(ref, ref, ag_s.at[g, b], r_sem, dev).start()

    def spread_first(g, b):
        for d in (2, 1, 3):
            pass_on(g, b, 0, a1_r.at[g, b, d - 1], at_y(d))
        pass_on(g, b, 0, fw_r.at[g, b], sib)

    def spread_from(g, b, d):
        received(had.at[g, chunk(b, c, 4 - d), :], a1_r.at[g, b, d - 1])
        pass_on(g, b, 4 - d, fw_r.at[g, b], sib)

    def spread_second(g, b):
        spread_from(g, b, 1)
        spread_from(g, b, 3)

    def spread_third(g, b):
        spread_from(g, b, 2)

    def spread_done(g, b):
        received(had.at[g, rows_at(base(b, 1 - c), 4 * OB[b]), :], fw_r.at[g, b])

    def zrow(b, d):
        return rows_at(8 * OFF[b] + ((z + d) % 8) * OB[b], OB[b])

    def norm_part(b):
        block = slice(8 * OFF[b], 8 * (OFF[b] + OB[b]))
        dn[block, :] = dot(had[1, block], wup[...])

    def zlanes(k, half):
        if not half:
            return slice(0, DW)
        return slice(0, CUT) if k == 0 else slice(CUT, DW)

    def hop(b, s):
        n = OB[b]
        for k, sign, to in ((0, -1, 1), (1, 1, 7)):
            mine = dn[zrow(b, 4 + sign * s), :]
            lanes = zlanes(k, s == 0)
            slot = k * 4 + s
            if s > 0:
                came = zlanes(k, s == 1)
                received(rb.at[b, slot - 1, 0:n, came], zr_r.at[b, slot - 1])
                if s == 1:
                    rest = zlanes(1 - k, True)
                    sb[b, slot, 0:n, rest] = mine[:, rest].astype(BF16)
                sb[b, slot, 0:n, came] = (mine[:, came] + rb[b, slot - 1, 0:n, came].astype(F32)).astype(BF16)
            else:
                sb[b, slot, 0:n, lanes] = mine[:, lanes].astype(BF16)
            send(
                sb.at[b, slot, 0:n, lanes], rb.at[b, slot, 0:n, lanes], zr_s.at[b], zr_r.at[b, slot], at_z(to)
            ).start()

    def land(b):
        n = OB[b]
        v = dn[zrow(b, 0), :]
        for k in range(2):
            received(rb.at[b, 4 * k + 3, 0:n], zr_r.at[b, 4 * k + 3])
            v = v + rb[b, 4 * k + 3, 0:n].astype(F32)
        xa[b, x, 0:n] = v.astype(BF16)
        ref = xa.at[b, x, 0:n]
        for d in (2, 1, 3):
            send(ref, ref, xe_s.at[b], xe_r.at[b], at_x(d)).start()

    def modul(b):
        rows = zrow(b, 0)
        gain = 1.0 + dot(oh[rows, :], rmod[1])
        rstd = col[1, rows, 0:1]
        xh = (tok[rows, :].astype(F32) - col[0, rows, 0:1]) * rstd
        return rows, gain, rstd, xh

    def finish_sums(b):
        n = OB[b]
        received(xa.at[b, 0:3, 0:n], xe_r.at[b])
        v = [xa[b, k, 0:n].astype(F32) for k in range(4)]
        v = (v[0] + v[1]) + (v[2] + v[3])
        rows, gain, rstd, xh = modul(b)
        dh = v * gain
        dhv[b, 0:n] = dh
        dhx = dh * xh
        s1 = dh[:, 0:128]
        s2 = dhx[:, 0:128]
        for k in range(1, 5):
            s1 = s1 + dh[:, k * 128 : (k + 1) * 128]
            s2 = s2 + dhx[:, k * 128 : (k + 1) * 128]
        both = [s1, s2] + [jnp.zeros((128 - 2 * n, 128), F32)] * (n < 64)
        both = jnp.concatenate(both, 0)
        mst[b, w] = jnp.sum(both.T, 0, keepdims=True)
        ref = mst.at[b, w]
        for d in range(1, 8):
            send(ref, ref, ms_s.at[b], ms_r.at[b], at_w(d)).start()

    def finish_rows(b):
        received(mst.at[b, 0:7], ms_r.at[b])
        n = OB[b]
        m = mst[b, 0]
        for k in range(1, 8):
            m = m + mst[b, k]
        mt = jnp.broadcast_to(m / D, (8, 128)).T
        rows, _, rstd, xh = modul(b)
        grad = cot[rows, :].astype(F32) + rstd * (dhv[b, 0:n] - mt[0:n, 0:1] - xh * mt[n : 2 * n, 0:1])
        gx[rows, :] = grad.astype(BF16)

    def ring(b, s):
        for k, sign, to in ((0, -1, 1), (1, 1, 7)):
            if s > 0:
                received(gx.at[zrow(b, 8 + sign * s), zlanes(k, s == 4)], zg_r.at[b, k, s - 1])
            if s < 4:
                ref = gx.at[zrow(b, 8 + sign * s), zlanes(k, s == 3)]
                send(ref, ref, zg_s.at[b], zg_r.at[b, k, s], at_z(to)).start()

    def table_block(b, carry):
        rows = rows_at(b * 128, 128, 128)
        dv = dn[rows, :]
        xh = (tok[rows, :].astype(F32) - col[0, rows, 0:1]) * col[1, rows, 0:1]
        yv = dot(had[0, rows, :], wdn[...]) * cot[rows, :].astype(F32)
        hot = oht[:, rows]
        out = []
        for acc, v in zip(carry, (dv, dv * xh, yv)):
            hi = v.astype(BF16)
            lo = (v - hi.astype(F32)).astype(BF16)
            out.append(acc + dot(hot, hi) + dot(hot, lo))
        return tuple(out)

    def kind_out(k):
        return send(
            tx.at[k, 3], tx.at[k, (x + 3 - k) % 4], tx_s.at[k], tx_r.at[0], (w, z * 4 + k)
        )

    def weight_gradient(out, left, right):
        for m in range(4):
            n = min(128, FW - m * 128)
            out[m * 128 : m * 128 + n, :] = dot(left[:, m * 128 : m * 128 + n], right[...], ((0,), (0,)))

    loads["seg"].wait()
    loads["cot"].wait()
    outer(0)
    loads["wdn"].wait()
    to_core(0, 0, dout, wdn)
    outer(1)
    to_core(0, 1, dout, wdn)
    to_chips(0, 0, dout, wdn)
    columns()
    normalize(0)
    loads["wup"].wait()
    to_core(1, 0, nrm, wup)
    to_chips(1, 0, nrm, wup)
    outer(2)
    to_core(0, 2, dout, wdn)
    to_chips(0, 1, dout, wdn)
    normalize(1)
    to_core(1, 1, nrm, wup)
    to_chips(1, 1, nrm, wup)
    loads["bias"].wait()
    activate(0)
    spread_first(1, 0)
    to_chips(0, 2, dout, wdn)
    normalize(2)
    to_core(1, 2, nrm, wup)
    to_chips(1, 2, nrm, wup)
    activate(1)
    spread_first(1, 1)
    spread_second(1, 0)
    spread_third(1, 0)
    spread_done(1, 0)
    norm_part(0)
    hop(0, 0)
    activate(2)
    spread_first(1, 2)
    spread_second(1, 1)
    spread_third(1, 1)
    hop(0, 1)
    spread_done(1, 1)
    norm_part(1)
    hop(1, 0)
    spread_second(1, 2)
    spread_third(1, 2)
    spread_first(0, 0)
    spread_first(0, 1)
    spread_first(0, 2)
    hop(0, 2)
    spread_done(1, 2)
    norm_part(2)
    hop(2, 0)
    hop(1, 1)
    hop(0, 3)
    hop(2, 1)
    hop(1, 2)
    land(0)
    spread_second(0, 0)
    spread_second(0, 1)
    spread_second(0, 2)
    hop(2, 2)
    hop(1, 3)
    finish_sums(0)
    spread_third(0, 0)
    spread_third(0, 1)
    spread_third(0, 2)
    land(1)
    hop(2, 3)
    finish_rows(0)
    ring(0, 0)
    spread_done(0, 0)
    spread_done(0, 1)
    spread_done(0, 2)
    zero = jnp.zeros((R, DW), F32)
    sums = lax.fori_loop(0, 4, table_block, (zero, zero, zero))
    finish_sums(1)
    land(2)
    ring(0, 1)
    sums = lax.fori_loop(4, 9, table_block, sums)

    for k in range(3):
        for q in range(8):
            tx[k, 3, q] = sums[k][2 * q : 2 * q + 2]
    for k in range(3):
        @pl.when(x != k)
        def _():
            kind_out(k).start()

    finish_rows(1)
    ring(1, 0)
    finish_sums(2)
    ring(0, 2)
    ring(1, 1)

    @pl.when(x < 3)
    def _():
        received(tx.at[0, 0:3], tx_r.at[0])
        tz[8] = (tx[x, 0] + tx[x, 1]) + (tx[x, 2] + tx[x, 3])
        for d in range(1, 8):
            send(tz.at[8, (z + d) % 8], tz.at[z, 0], tz_s.at[0], tz_r.at[0], at_z(d)).start()

    finish_rows(2)
    ring(2, 0)
    ring(0, 3)
    ring(1, 2)

    @pl.when(x < 3)
    def _():
        received(tz.at[0:7, 0], tz_r.at[0])
        sent(tz.at[0:7, 0], tz_s.at[0])
        tz[z, 0] = tz[8, z]
        v = tz[0, 0]
        for k in range(1, 8):
            v = v + tz[k, 0]
        tf[x, z] = v
        for d in range(1, 8):
            send(tf.at[x, z], tf.at[x, z], tg_s.at[0], tg_r.at[0], at_z(d)).start()

    ring(2, 1)
    ring(1, 3)

    @pl.when(x < 3)
    def _():
        received(tf.at[x, 0:7], tg_r.at[0])
        sent(tf.at[x, 0:7], tg_s.at[0])
        for d in range(1, 4):
            send(tf.at[x], tf.at[x], tb_s.at[0], tb_r.at[x], at_x(d)).start()

    ring(2, 2)
    weight_gradient(gdn, had[0], dout)
    weight_gradient(gup, had[1], nrm)
    ring(2, 3)
    gb[...] = dot(jnp.ones((8, T), BF16), had[1])[0:1]
    sent(stat.at[0:7], st_s.at[0])
    for b in range(NB):
        n = OB[b]
        for a in range(2):
            sent(psib.at[a, 0 : 3 * n], y_s.at[a, b])
            sent(had.at[a, 0 : 7 * n], ag_s.at[a, b])
        sent(sb.at[b, 0:7, 0:n], zr_s.at[b])
        sent(xa.at[b, 0:3, 0:n], xe_s.at[b])
        sent(mst.at[b, 0:7], ms_s.at[b])

    for k in range(3):
        @pl.when(x != k)
        def _():
            received(tf.at[k], tb_r.at[k])
            kind_out(k).wait_send()

    @pl.when(x < 3)
    def _():
        sent(tf.at[0:3], tb_s.at[0])

    for k in range(3):
        for q in range(8):
            comp[k, 2 * q : 2 * q + 2, :] = tf[k, q]
        out = jnp.zeros((NS, DW), F32)
        for p in split3(comp[k]):
            out = out + dot(step_of, p)
        gtab[k] = out

    for b in range(NB):
        ring(b, 4)
        sent(gx.at[0 : 7 * OB[b]], zg_s.at[b])


def flush(*refs):
    copies = [pltpu.make_async_copy(refs[k], refs[5 + k], refs[10].at[k]) for k in range(5)]
    for cp in copies:
        cp.start()
    for cp in copies:
        cp.wait()


def per_device(tokens, cotangent, w_up, bias_up, w_down, mod_table, seg_ids, step_ids):
    vm = pl.BlockSpec(memory_space=pltpu.VMEM)
    hbm = pl.BlockSpec(memory_space=pltpu.HBM)
    dma = pltpu.SemaphoreType.DMA
    shapes = (
        jax.ShapeDtypeStruct((T, DW), BF16),
        jax.ShapeDtypeStruct((FW, DW), F32),
        jax.ShapeDtypeStruct((FW, DW), F32),
        jax.ShapeDtypeStruct((1, FW), F32),
        jax.ShapeDtypeStruct((3, NS, DW), F32),
    )
    outs = pl.pallas_call(
        kernel,
        out_shape=shapes,
        in_specs=[hbm] * 8,
        out_specs=(vm,) * 5,
        scratch_shapes=[
            pltpu.VMEM((T, DW), BF16),
            pltpu.VMEM((T, DW), BF16),
            pltpu.VMEM((FW, DW), BF16),
            pltpu.VMEM((1, FW), F32),
            pltpu.VMEM((FW, DW), BF16),
            pltpu.VMEM((3, NS, DW), F32),
            pltpu.VMEM((T,), jnp.int32),
            pltpu.VMEM((R,), jnp.int32),
            pltpu.VMEM((8, 2, T), F32),
            pltpu.VMEM((3, 3 * R, DW), BF16),
            pltpu.VMEM((T, 3 * R), BF16),
            pltpu.VMEM((R, T), BF16),
            pltpu.VMEM((2, T, 8), F32),
            pltpu.VMEM((T, DW), BF16),
            pltpu.VMEM((T, DW), BF16),
            pltpu.VMEM((2, 4 * CH, FW), BF16),
            pltpu.VMEM((2, 4 * CH, FW), BF16),
            pltpu.VMEM((2, 4 * CH, FW), F32),
            pltpu.VMEM((2, 3, CH, FW), BF16),
            pltpu.VMEM((2, 3, CH, FW), BF16),
            pltpu.VMEM((2, T, FW), BF16),
            pltpu.VMEM((T, DW), F32),
            pltpu.VMEM((NB, 8, max(OB), DW), BF16),
            pltpu.VMEM((NB, 8, max(OB), DW), BF16),
            pltpu.VMEM((NB, 4, max(OB), DW), BF16),
            pltpu.VMEM((NB, max(OB), DW), F32),
            pltpu.VMEM((NB, 8, 1, 128), F32),
            pltpu.VMEM((3, 4, 8, 2, DW), F32),
            pltpu.VMEM((9, 8, 2, DW), F32),
            pltpu.VMEM((3, 8, 2, DW), F32),
            pltpu.VMEM((3, R, DW), F32),
            dma((8,)),
            dma((1,)), dma((1,)),
            dma((2, NB)), dma((2, NB)),
            dma((2, NB)), dma((2, NB, 3)),
            dma((2, NB)), dma((2, NB, 3)), dma((2, NB)),
            dma((NB,)), dma((NB, 8)),
            dma((NB,)), dma((NB,)),
            dma((NB,)), dma((NB,)),
            dma((NB,)), dma((NB, 2, 4)),
            dma((3,)), dma((1,)),
            dma((1,)), dma((1,)),
            dma((1,)), dma((1,)),
            dma((1,)), dma((3,)),
        ],
        compiler_params=pltpu.CompilerParams(
            collective_id=0, has_side_effects=True, vmem_limit_bytes=34 * 1024 * 1024
        ),
        name="mlp_backward",
    )(
        *(
            pltpu.with_memory_space_constraint(v, pltpu.HBM)
            for v in (tokens, cotangent, w_up.T, bias_up[None, :], w_down, mod_table.transpose(1, 0, 2), seg_ids, step_ids)
        ),
    )
    outs = pl.pallas_call(
        flush,
        out_shape=shapes,
        in_specs=[vm] * 5,
        out_specs=(hbm,) * 5,
        scratch_shapes=[dma((5,))],
        compiler_params=pltpu.CompilerParams(vmem_limit_bytes=1024 * 1024),
        name="write_out",
    )(*outs)
    return outs[0], outs[1].T, outs[2], outs[3][0], outs[4].transpose(1, 0, 2)


def solution(mesh):
    placed = (
        P(None, "width"),
        P(None, "width"),
        P("width", "hidden"),
        P("hidden"),
        P("hidden", "width"),
        P(None, None, "width"),
        P(),
        P(),
    )
    return jax.shard_map(
        per_device,
        mesh=mesh,
        in_specs=placed,
        out_specs=(
            P(None, "width"),
            P("width", "hidden"),
            P("hidden", "width"),
            P("hidden"),
            P(None, None, "width"),
        ),
        check_vma=False,
    )
```

```python
import functools

import jax
import jax.numpy as jnp
from jax import lax
from jax.experimental import pallas as pl
from jax.experimental.pallas import tpu as pltpu
from jax.sharding import PartitionSpec as P

MESH = pl.DeviceIdType.MESH
F32, BF16 = jnp.float32, jnp.bfloat16

T, DW, FW, R, NS = 1152, 640, 432, 16, 32
D = 5120
UNITS = (3, 3, 3)
NB = len(UNITS)
OB = tuple(16 * u for u in UNITS)
OFF = tuple(sum(OB[:b]) for b in range(NB))
CH = sum(OB)
CUT = 384
ROOT = 0.7978845608028654
CUBE = 0.044715


def split3(v):
    hi = v.astype(BF16)
    rest = v - hi.astype(F32)
    mid = rest.astype(BF16)
    return hi, mid, (rest - mid.astype(F32)).astype(BF16)


def dot(a, b, dims=((1,), (0,))):
    return lax.dot_general(a, b, (dims, ((), ())), preferred_element_type=F32)


def rows_at(start, size, step=16):
    return pl.ds(pl.multiple_of(start, step), size)


def kernel(
    tok_h, cot_h, wup_h, bias_h, wdn_h, tab_h, seg_h, stp_h,
    gx, gup, gdn, gb, gtab,
    tok, cot, wup, bias, wdn, tab, seg, stp,
    stat, rmod, oh, oht, col, dout, nrm,
    psib, rsib, pown, ys, yr, had,
    dn, sb, rb, xa, dhv, mst,
    tx, tz, tf, comp,
    in_s, st_s, st_r, cx_s, cx_r, y_s, yr_r, ag_s, a1_r, fw_r,
    zr_s, zr_r, xe_s, xe_r, ms_s, ms_r, zg_s, zg_r,
    tx_s, tx_r, tz_s, tz_r, tg_s, tg_r, tb_s, tb_r,
):
    w = lax.axis_index("width")
    h = lax.axis_index("hidden")
    y, c = w // 2, w % 2
    z, x = h // 4, h % 4

    def at_w(d):
        return ((w + d) % 8, h)

    def at_y(d):
        return (((y + d) % 4) * 2 + c, h)

    sib = (y * 2 + 1 - c, h)

    def at_z(d):
        return (w, ((z + d) % 8) * 4 + x)

    def at_x(d):
        return (w, z * 4 + (x + d) % 4)

    def send(src, dst, s_sem, r_sem, dev):
        return pltpu.make_async_remote_copy(
            src_ref=src, dst_ref=dst, send_sem=s_sem, recv_sem=r_sem, device_id=dev, device_id_type=MESH
        )

    def received(ref, sem):
        send(ref, ref, sem, sem, sib).wait_recv()

    def sent(ref, sem):
        send(ref, ref, sem, sem, sib).wait_send()

    loads = {}
    for i, (name, src, dst) in enumerate(
        (
            ("tok", tok_h, tok), ("stp", stp_h, stp), ("tab", tab_h, tab), ("seg", seg_h, seg), ("cot", cot_h, cot),
            ("wdn", wdn_h, wdn), ("wup", wup_h, wup), ("bias", bias_h, bias),
        )
    ):
        loads[name] = pltpu.make_async_copy(src, dst, in_s.at[i])
        loads[name].start()

    bar = pltpu.get_barrier_semaphore()
    for d in range(1, 8):
        pl.semaphore_signal(bar, inc=1, device_id=at_w(d), device_id_type=MESH)
        pl.semaphore_signal(bar, inc=1, device_id=at_z(d), device_id_type=MESH)
    for d in range(1, 4):
        pl.semaphore_signal(bar, inc=1, device_id=at_x(d), device_id_type=MESH)

    loads["tok"].wait()

    @pl.loop(0, 9)
    def _(b):
        v = tok[rows_at(b * 128, 128, 128), :].astype(F32)
        s1 = v[:, 0:128]
        s2 = v[:, 0:128] * v[:, 0:128]
        for k in range(1, 5):
            p = v[:, k * 128 : (k + 1) * 128]
            s1 = s1 + p
            s2 = s2 + p * p
        lanes = rows_at(b * 128, 128, 128)
        stat[w, 0:1, lanes] = jnp.sum(s1.T, 0, keepdims=True)
        stat[w, 1:2, lanes] = jnp.sum(s2.T, 0, keepdims=True)

    pl.semaphore_wait(bar, 17)
    for d in range(1, 8):
        send(stat.at[w], stat.at[w], st_s.at[0], st_r.at[0], at_w(d)).start()

    loads["stp"].wait()
    ids = jnp.broadcast_to(stp[...].reshape(1, R), (NS, R))
    step_of = (ids == lax.broadcasted_iota(jnp.int32, (NS, R), 0)).astype(F32).astype(BF16)
    loads["tab"].wait()
    for k in range(3):
        parts = split3(tab[k])
        rm = sum(dot(step_of, piece, ((0,), (0,))) for piece in parts)
        for i, piece in enumerate(split3(rm)):
            rmod[k, i * R : (i + 1) * R, :] = piece

    def units(b):
        return sum(UNITS[:b]), sum(UNITS[: b + 1])

    def outer(b):
        @pl.loop(*units(b))
        def _(i):
            lanes = rows_at(i * 128, 128, 128)
            ids = jnp.broadcast_to(seg[lanes].reshape(1, 128), (R, 128))
            one = (ids == lax.broadcasted_iota(jnp.int32, (R, 128), 0)).astype(F32)
            oht[:, lanes] = one.astype(BF16)
            three = jnp.concatenate([one, one, one], 0)
            oh[lanes, :] = three.T.astype(BF16)
            gate = dot(oh[lanes, :], rmod[2])
            dout[lanes, :] = (cot[lanes, :].astype(F32) * gate).astype(BF16)

    def base(b, k):
        return 8 * OFF[b] + k * 4 * OB[b]

    def part(b):
        return slice(OFF[b], OFF[b] + OB[b])

    def four(b):
        return slice(4 * OFF[b], 4 * OFF[b] + 4 * OB[b])

    def target(b, d):
        return rows_at(4 * OFF[b] + ((y + d) % 4) * OB[b], OB[b])

    cx = {}

    def to_core(a, b, left, right):
        psib[a, four(b)] = dot(left[rows_at(base(b, 1 - c), 4 * OB[b]), :], right[...], ((1,), (1,))).astype(BF16)
        cx[a, b] = send(psib.at[a, four(b)], rsib.at[a, four(b)], cx_s.at[a, b], cx_r.at[a, b], sib)
        cx[a, b].start()

    def to_chips(a, b, left, right):
        p = dot(left[rows_at(base(b, c), 4 * OB[b]), :], right[...], ((1,), (1,)))
        cx[a, b].wait()
        pown[a, four(b)] = p + rsib[a, four(b)].astype(F32)
        for d in (2, 1, 3):
            ys[a, d - 1, part(b)] = pown[a, target(b, d), :].astype(BF16)
            send(
                ys.at[a, d - 1, part(b)], yr.at[a, d - 1, part(b)], y_s.at[a, b], yr_r.at[a, b, d - 1], at_y(d)
            ).start()

    def columns():
        received(stat.at[0:7], st_r.at[0])
        tot = stat[0]
        for k in range(1, 8):
            tot = tot + stat[k]
        mu = tot[0:1] / D
        inv = lax.rsqrt(tot[1:2] / D - mu * mu + 1e-06)
        mu8 = jnp.broadcast_to(mu, (8, T))
        inv8 = jnp.broadcast_to(inv, (8, T))
        for b in range(9):
            lanes = slice(b * 128, (b + 1) * 128)
            col[0, lanes, :] = mu8[:, lanes].T
            col[1, lanes, :] = inv8[:, lanes].T

    def normalize(b):
        @pl.loop(*units(b))
        def _(i):
            rows = rows_at(i * 128, 128, 128)
            shift = dot(oh[rows, :], rmod[0])
            gain = 1.0 + dot(oh[rows, :], rmod[1])
            xh = (tok[rows, :].astype(F32) - col[0, rows, 0:1]) * col[1, rows, 0:1]
            nrm[rows, :] = (xh * gain + shift).astype(BF16)

    def total(a, b):
        v = pown[a, target(b, 0), :]
        for k in range(3):
            v = v + yr[a, k, part(b)].astype(F32)
        return v

    def chunk(b, k, d):
        return rows_at(base(b, k) + ((y + d) % 4) * OB[b], OB[b])

    def activate(b):
        for a in range(2):
            for k in range(3):
                received(yr.at[a, k, part(b)], yr_r.at[a, b, k])
        pre = total(1, b) + bias[...]
        sq = pre * pre
        th = jnp.tanh(ROOT * (pre + CUBE * (sq * pre)))
        slope = 0.5 * (1.0 + th) + (0.5 * ROOT) * pre * (1.0 - th * th) * (1.0 + (3.0 * CUBE) * sq)
        had[1, chunk(b, c, 0), :] = (total(0, b) * slope).astype(BF16)
        had[0, chunk(b, c, 0), :] = (0.5 * pre * (1.0 + th)).astype(BF16)

    def pass_on(g, b, d, r_sem, dev):
        ref = had.at[g, chunk(b, c, d), :]
        send(ref, ref, ag_s.at[g, b], r_sem, dev).start()

    def spread_first(g, b):
        for d in (2, 1, 3):
            pass_on(g, b, 0, a1_r.at[g, b, d - 1], at_y(d))
        pass_on(g, b, 0, fw_r.at[g, b], sib)

    def spread_from(g, b, d):
        received(had.at[g, chunk(b, c, 4 - d), :], a1_r.at[g, b, d - 1])
        pass_on(g, b, 4 - d, fw_r.at[g, b], sib)

    def spread_second(g, b):
        spread_from(g, b, 1)
        spread_from(g, b, 3)

    def spread_third(g, b):
        spread_from(g, b, 2)

    def spread_done(g, b):
        received(had.at[g, rows_at(base(b, 1 - c), 4 * OB[b]), :], fw_r.at[g, b])

    def zrow(b, d):
        return rows_at(8 * OFF[b] + ((z + d) % 8) * OB[b], OB[b])

    def norm_part(b):
        block = slice(8 * OFF[b], 8 * (OFF[b] + OB[b]))
        dn[block, :] = dot(had[1, block], wup[...])

    def zlanes(k, half):
        if not half:
            return slice(0, DW)
        return slice(0, CUT) if k == 0 else slice(CUT, DW)

    def hop(b, s):
        n = OB[b]
        for k, sign, to in ((0, -1, 1), (1, 1, 7)):
            mine = dn[zrow(b, 4 + sign * s), :]
            lanes = zlanes(k, s == 0)
            slot = k * 4 + s
            if s > 0:
                came = zlanes(k, s == 1)
                received(rb.at[b, slot - 1, 0:n, came], zr_r.at[b, slot - 1])
                if s == 1:
                    rest = zlanes(1 - k, True)
                    sb[b, slot, 0:n, rest] = mine[:, rest].astype(BF16)
                sb[b, slot, 0:n, came] = (mine[:, came] + rb[b, slot - 1, 0:n, came].astype(F32)).astype(BF16)
            else:
                sb[b, slot, 0:n, lanes] = mine[:, lanes].astype(BF16)
            send(
                sb.at[b, slot, 0:n, lanes], rb.at[b, slot, 0:n, lanes], zr_s.at[b], zr_r.at[b, slot], at_z(to)
            ).start()

    def land(b):
        n = OB[b]
        v = dn[zrow(b, 0), :]
        for k in range(2):
            received(rb.at[b, 4 * k + 3, 0:n], zr_r.at[b, 4 * k + 3])
            v = v + rb[b, 4 * k + 3, 0:n].astype(F32)
        xa[b, x, 0:n] = v.astype(BF16)
        ref = xa.at[b, x, 0:n]
        for d in (2, 1, 3):
            send(ref, ref, xe_s.at[b], xe_r.at[b], at_x(d)).start()

    def modul(b):
        rows = zrow(b, 0)
        gain = 1.0 + dot(oh[rows, :], rmod[1])
        rstd = col[1, rows, 0:1]
        xh = (tok[rows, :].astype(F32) - col[0, rows, 0:1]) * rstd
        return rows, gain, rstd, xh

    def finish_sums(b):
        n = OB[b]
        rows, gain, rstd, xh = modul(b)
        received(xa.at[b, 0:3, 0:n], xe_r.at[b])
        v = [xa[b, k, 0:n].astype(F32) for k in range(4)]
        v = (v[0] + v[1]) + (v[2] + v[3])
        dh = v * gain
        dhv[b, 0:n] = dh
        dhx = dh * xh
        s1 = dh[:, 0:128]
        s2 = dhx[:, 0:128]
        for k in range(1, 5):
            s1 = s1 + dh[:, k * 128 : (k + 1) * 128]
            s2 = s2 + dhx[:, k * 128 : (k + 1) * 128]
        both = [s1, s2] + [jnp.zeros((128 - 2 * n, 128), F32)] * (n < 64)
        both = jnp.concatenate(both, 0)
        mst[b, w] = jnp.sum(both.T, 0, keepdims=True)
        ref = mst.at[b, w]
        for d in range(1, 8):
            send(ref, ref, ms_s.at[b], ms_r.at[b], at_w(d)).start()

    def finish_rows(b):
        n = OB[b]
        rows, _, rstd, xh = modul(b)
        received(mst.at[b, 0:7], ms_r.at[b])
        m = mst[b, 0]
        for k in range(1, 8):
            m = m + mst[b, k]
        mt = jnp.broadcast_to(m / D, (8, 128)).T
        grad = cot[rows, :].astype(F32) + rstd * (dhv[b, 0:n] - mt[0:n, 0:1] - xh * mt[n : 2 * n, 0:1])
        gx[rows, :] = grad.astype(BF16)

    def ring(b, s):
        for k, sign, to in ((0, -1, 1), (1, 1, 7)):
            if s > 0:
                received(gx.at[zrow(b, 8 + sign * s), zlanes(k, s == 4)], zg_r.at[b, k, s - 1])
            if s < 4:
                ref = gx.at[zrow(b, 8 + sign * s), zlanes(k, s == 3)]
                send(ref, ref, zg_s.at[b], zg_r.at[b, k, s], at_z(to)).start()

    def table_block(b, carry):
        rows = rows_at(b * 128, 128, 128)
        dv = dn[rows, :]
        xh = (tok[rows, :].astype(F32) - col[0, rows, 0:1]) * col[1, rows, 0:1]
        yv = dot(had[0, rows, :], wdn[...]) * cot[rows, :].astype(F32)
        hot = oht[:, rows]
        out = []
        for acc, v in zip(carry, (dv, dv * xh, yv)):
            hi = v.astype(BF16)
            lo = (v - hi.astype(F32)).astype(BF16)
            out.append(acc + dot(hot, hi) + dot(hot, lo))
        return tuple(out)

    def kind_out(k):
        return send(
            tx.at[k, 3], tx.at[k, (x + 3 - k) % 4], tx_s.at[k], tx_r.at[0], (w, z * 4 + k)
        )

    def weight_gradient(out, left, right):
        for m in range(4):
            n = min(128, FW - m * 128)
            out[m * 128 : m * 128 + n, :] = dot(left[:, m * 128 : m * 128 + n], right[...], ((0,), (0,)))

    loads["seg"].wait()
    loads["cot"].wait()
    outer(0)
    loads["wdn"].wait()
    to_core(0, 0, dout, wdn)
    outer(1)
    to_core(0, 1, dout, wdn)
    to_chips(0, 0, dout, wdn)
    columns()
    normalize(0)
    loads["wup"].wait()
    to_core(1, 0, nrm, wup)
    to_chips(1, 0, nrm, wup)
    outer(2)
    to_core(0, 2, dout, wdn)
    to_chips(0, 1, dout, wdn)
    normalize(1)
    to_core(1, 1, nrm, wup)
    to_chips(1, 1, nrm, wup)
    loads["bias"].wait()
    activate(0)
    spread_first(1, 0)
    to_chips(0, 2, dout, wdn)
    normalize(2)
    to_core(1, 2, nrm, wup)
    to_chips(1, 2, nrm, wup)
    activate(1)
    spread_first(1, 1)
    spread_second(1, 0)
    spread_third(1, 0)
    spread_done(1, 0)
    norm_part(0)
    hop(0, 0)
    activate(2)
    spread_first(1, 2)
    spread_second(1, 1)
    spread_third(1, 1)
    hop(0, 1)
    spread_done(1, 1)
    norm_part(1)
    hop(1, 0)
    spread_second(1, 2)
    spread_third(1, 2)
    spread_first(0, 0)
    spread_first(0, 1)
    spread_first(0, 2)
    hop(0, 2)
    spread_done(1, 2)
    norm_part(2)
    hop(2, 0)
    hop(1, 1)
    hop(0, 3)
    hop(2, 1)
    hop(1, 2)
    land(0)
    spread_second(0, 0)
    spread_second(0, 1)
    spread_second(0, 2)
    hop(2, 2)
    hop(1, 3)
    finish_sums(0)
    spread_third(0, 0)
    spread_third(0, 1)
    spread_third(0, 2)
    land(1)
    hop(2, 3)
    finish_rows(0)
    ring(0, 0)
    spread_done(0, 0)
    spread_done(0, 1)
    spread_done(0, 2)
    zero = jnp.zeros((R, DW), F32)
    sums = lax.fori_loop(0, 4, table_block, (zero, zero, zero))
    finish_sums(1)
    land(2)
    ring(0, 1)
    sums = lax.fori_loop(4, 9, table_block, sums)

    for k in range(3):
        for q in range(8):
            tx[k, 3, q] = sums[k][2 * q : 2 * q + 2]
    for k in range(3):
        @pl.when(x != k)
        def _():
            kind_out(k).start()

    finish_rows(1)
    ring(1, 0)
    finish_sums(2)
    ring(0, 2)
    ring(1, 1)

    @pl.when(x < 3)
    def _():
        received(tx.at[0, 0:3], tx_r.at[0])
        tz[8] = (tx[x, 0] + tx[x, 1]) + (tx[x, 2] + tx[x, 3])
        for d in range(1, 8):
            send(tz.at[8, (z + d) % 8], tz.at[z, 0], tz_s.at[0], tz_r.at[0], at_z(d)).start()

    finish_rows(2)
    ring(2, 0)
    ring(0, 3)
    ring(1, 2)

    @pl.when(x < 3)
    def _():
        received(tz.at[0:7, 0], tz_r.at[0])
        sent(tz.at[0:7, 0], tz_s.at[0])
        tz[z, 0] = tz[8, z]
        v = tz[0, 0]
        for k in range(1, 8):
            v = v + tz[k, 0]
        tf[x, z] = v
        for d in range(1, 8):
            send(tf.at[x, z], tf.at[x, z], tg_s.at[0], tg_r.at[0], at_z(d)).start()

    ring(2, 1)
    ring(1, 3)

    @pl.when(x < 3)
    def _():
        received(tf.at[x, 0:7], tg_r.at[0])
        sent(tf.at[x, 0:7], tg_s.at[0])
        for d in range(1, 4):
            send(tf.at[x], tf.at[x], tb_s.at[0], tb_r.at[x], at_x(d)).start()

    ring(2, 2)
    weight_gradient(gdn, had[0], dout)
    weight_gradient(gup, had[1], nrm)
    ring(2, 3)
    gb[...] = dot(jnp.ones((8, T), BF16), had[1])[0:1]
    sent(stat.at[0:7], st_s.at[0])
    for b in range(NB):
        n = OB[b]
        for a in range(2):
            sent(psib.at[a, 0 : 3 * n], y_s.at[a, b])
            sent(had.at[a, 0 : 7 * n], ag_s.at[a, b])
        sent(sb.at[b, 0:7, 0:n], zr_s.at[b])
        sent(xa.at[b, 0:3, 0:n], xe_s.at[b])
        sent(mst.at[b, 0:7], ms_s.at[b])

    for k in range(3):
        @pl.when(x != k)
        def _():
            received(tf.at[k], tb_r.at[k])
            kind_out(k).wait_send()

    @pl.when(x < 3)
    def _():
        sent(tf.at[0:3], tb_s.at[0])

    for k in range(3):
        for q in range(8):
            comp[k, 2 * q : 2 * q + 2, :] = tf[k, q]
        out = jnp.zeros((NS, DW), F32)
        for p in split3(comp[k]):
            out = out + dot(step_of, p)
        gtab[k] = out

    for b in range(NB):
        ring(b, 4)
        sent(gx.at[0 : 7 * OB[b]], zg_s.at[b])


def flush(*refs):
    copies = [pltpu.make_async_copy(refs[k], refs[5 + k], refs[10].at[k]) for k in range(5)]
    for cp in copies:
        cp.start()
    for cp in copies:
        cp.wait()


def per_device(tokens, cotangent, w_up, bias_up, w_down, mod_table, seg_ids, step_ids):
    vm = pl.BlockSpec(memory_space=pltpu.VMEM)
    hbm = pl.BlockSpec(memory_space=pltpu.HBM)
    dma = pltpu.SemaphoreType.DMA
    shapes = (
        jax.ShapeDtypeStruct((T, DW), BF16),
        jax.ShapeDtypeStruct((FW, DW), F32),
        jax.ShapeDtypeStruct((FW, DW), F32),
        jax.ShapeDtypeStruct((1, FW), F32),
        jax.ShapeDtypeStruct((3, NS, DW), F32),
    )
    outs = pl.pallas_call(
        kernel,
        out_shape=shapes,
        in_specs=[hbm] * 8,
        out_specs=(vm,) * 5,
        scratch_shapes=[
            pltpu.VMEM((T, DW), BF16),
            pltpu.VMEM((T, DW), BF16),
            pltpu.VMEM((FW, DW), BF16),
            pltpu.VMEM((1, FW), F32),
            pltpu.VMEM((FW, DW), BF16),
            pltpu.VMEM((3, NS, DW), F32),
            pltpu.VMEM((T,), jnp.int32),
            pltpu.VMEM((R,), jnp.int32),
            pltpu.VMEM((8, 2, T), F32),
            pltpu.VMEM((3, 3 * R, DW), BF16),
            pltpu.VMEM((T, 3 * R), BF16),
            pltpu.VMEM((R, T), BF16),
            pltpu.VMEM((2, T, 8), F32),
            pltpu.VMEM((T, DW), BF16),
            pltpu.VMEM((T, DW), BF16),
            pltpu.VMEM((2, 4 * CH, FW), BF16),
            pltpu.VMEM((2, 4 * CH, FW), BF16),
            pltpu.VMEM((2, 4 * CH, FW), F32),
            pltpu.VMEM((2, 3, CH, FW), BF16),
            pltpu.VMEM((2, 3, CH, FW), BF16),
            pltpu.VMEM((2, T, FW), BF16),
            pltpu.VMEM((T, DW), F32),
            pltpu.VMEM((NB, 8, max(OB), DW), BF16),
            pltpu.VMEM((NB, 8, max(OB), DW), BF16),
            pltpu.VMEM((NB, 4, max(OB), DW), BF16),
            pltpu.VMEM((NB, max(OB), DW), F32),
            pltpu.VMEM((NB, 8, 1, 128), F32),
            pltpu.VMEM((3, 4, 8, 2, DW), F32),
            pltpu.VMEM((9, 8, 2, DW), F32),
            pltpu.VMEM((3, 8, 2, DW), F32),
            pltpu.VMEM((3, R, DW), F32),
            dma((8,)),
            dma((1,)), dma((1,)),
            dma((2, NB)), dma((2, NB)),
            dma((2, NB)), dma((2, NB, 3)),
            dma((2, NB)), dma((2, NB, 3)), dma((2, NB)),
            dma((NB,)), dma((NB, 8)),
            dma((NB,)), dma((NB,)),
            dma((NB,)), dma((NB,)),
            dma((NB,)), dma((NB, 2, 4)),
            dma((3,)), dma((1,)),
            dma((1,)), dma((1,)),
            dma((1,)), dma((1,)),
            dma((1,)), dma((3,)),
        ],
        compiler_params=pltpu.CompilerParams(
            collective_id=0, has_side_effects=True, vmem_limit_bytes=34 * 1024 * 1024
        ),
        name="mlp_backward",
    )(
        *(
            pltpu.with_memory_space_constraint(v, pltpu.HBM)
            for v in (tokens, cotangent, w_up.T, bias_up[None, :], w_down, mod_table.transpose(1, 0, 2), seg_ids, step_ids)
        ),
    )
    outs = pl.pallas_call(
        flush,
        out_shape=shapes,
        in_specs=[vm] * 5,
        out_specs=(hbm,) * 5,
        scratch_shapes=[dma((5,))],
        compiler_params=pltpu.CompilerParams(vmem_limit_bytes=1024 * 1024),
        name="write_out",
    )(*outs)
    return outs[0], outs[1].T, outs[2], outs[3][0], outs[4].transpose(1, 0, 2)


def solution(mesh):
    placed = (
        P(None, "width"),
        P(None, "width"),
        P("width", "hidden"),
        P("hidden"),
        P("hidden", "width"),
        P(None, None, "width"),
        P(),
        P(),
    )
    return jax.shard_map(
        per_device,
        mesh=mesh,
        in_specs=placed,
        out_specs=(
            P(None, "width"),
            P("width", "hidden"),
            P("hidden", "width"),
            P("hidden"),
            P(None, None, "width"),
        ),
        check_vma=False,
    )
```
